32 devices in a mesh: row: 4 (over z), col: 8 (over y, x, core).
Axes of the slice: x: 2, y: 2, z: 4, core: 2. Of those that a mesh axis runs over, the one named last changes fastest.
Arguments:
- pair_state: bfloat16 [384, 384, 128], P('row', 'col'), may hold values from -40 to 40
- seq_state: bfloat16 [384, 1024], P('row', 'col'), may hold values from -40 to 40
- residue_index: int32 [384], replicated, may hold values from 0 to 1535, as said below
- residue_mask: int32 [384], replicated, may hold values from 0 to 1, as said below
- position_table: bfloat16 [66, 128], replicated, may hold values from -4 to 4
- attention_gain: float32 [2, 1024], replicated, may hold values from 0.1 to 1.9
- bias_norm_gain: float32 [2, 128], replicated, may hold values from 0.1 to 1.9
- query_weight: bfloat16 [2, 1024, 1024], P(None, None, 'col'), may hold values from -16 to 16
- key_weight: bfloat16 [2, 1024, 1024], P(None, None, 'col'), may hold values from -1 to 1
- value_weight: bfloat16 [2, 1024, 1024], P(None, None, 'col'), may hold values from -0.1875 to 0.1875
- gate_weight: bfloat16 [2, 1024, 1024], P(None, None, 'col'), may hold values from -0.1875 to 0.1875
- out_weight: bfloat16 [2, 1024, 1024], P(None, None, 'col'), may hold values from -0.75 to 0.75
- bias_weight: bfloat16 [2, 128, 32], replicated, may hold values from -1.5 to 1.5
- outer_gain: float32 [2, 1024], replicated, may hold values from 0.1 to 1.9
- outer_weight: bfloat16 [2, 1024, 128], replicated, may hold values from -0.1875 to 0.1875
- outer_out_weight: bfloat16 [2, 128, 128], replicated, may hold values from -0.5 to 0.5
- transition_gain: float32 [2, 128], replicated, may hold values from 0.1 to 1.9
- up_weight: bfloat16 [2, 128, 512], replicated, may hold values from -0.5 to 0.5
- down_weight: bfloat16 [2, 512, 128], replicated, may hold values from -0.25 to 0.25
- distance_weight: bfloat16 [128, 64], replicated, may hold values from -0.5 to 0.5
Outputs:
- distogram: bfloat16 [384, 384, 64], P('row', 'col')
- seq_out: bfloat16 [384, 1024], P('row', 'col')
The draws below stay inside these ranges and needn't reach their ends.
Inputs may be any that keep to these rules, and one draw needn't show every extreme that they name: `residue_index`: strictly increasing; the first entry is 0 and the last is 1535. `residue_mask`: 1 on a prefix of 192 to 383 residues and 0 after it.
All inputs are finite; a program needn't handle non-finite values.
Results may differ from the reference program's by a relative error of at most 0.028.
Values may be sent and summed in bfloat16 or wider, within the bound.
A program may use at most 64 MiB of HBM per device.

```python
import jax
import jax.numpy as jnp
from jax import lax

CS = 1024
HEAD_DIM = 32
CZ = 128
BINS = 64
RELPOS_MAX = 32
LAYERS = 2
HEADS = 32
INNER = 64
FFZ = 512
RELPOS_BINS = 66
LENGTH = 384
N_ROW = 4


def draw_pair_state(key, part):
    base_key = jax.random.fold_in(jax.random.fold_in(key, 1), 0)
    values = jax.random.truncated_normal(base_key, -4.0, 4.0, (LENGTH, LENGTH, CZ), jnp.float32)
    return values.astype(jnp.bfloat16)


def draw_seq_state(key, part):
    base_key = jax.random.fold_in(jax.random.fold_in(key, 2), 0)
    values = jax.random.truncated_normal(base_key, -4.0, 4.0, (LENGTH, CS), jnp.float32)
    return values.astype(jnp.bfloat16)


def attention_pair(key):
    key_first, key_second = jax.random.split(jax.random.fold_in(key, 7), 2)
    shaped = (LAYERS, CS, CS)
    key_part = jax.random.truncated_normal(key_first, -4.0, 4.0, shaped, jnp.float32) * CS ** (-0.5)
    noise_part = jax.random.truncated_normal(key_second, -4.0, 4.0, shaped, jnp.float32) * CS ** (-0.5)
    return (key_part, noise_part)


def draw_key_weight(key, part):
    key_part, noise_part = attention_pair(key)
    return key_part.astype(jnp.bfloat16)


def draw_query_weight(key, part):
    key_part, noise_part = attention_pair(key)
    return noise_part.astype(jnp.bfloat16)


def draw_residue_mask(key, part):
    live_count = jax.random.randint(jax.random.fold_in(key, 3), (), LENGTH // 2, LENGTH)
    return (jnp.arange(LENGTH, dtype=jnp.int32) < live_count).astype(jnp.int32)


def draw_residue_index(key, part):
    inner_count = 4 * LENGTH - 2
    chosen = jax.random.permutation(jax.random.fold_in(key, 5), inner_count)[:LENGTH - 2].astype(jnp.int32) + 1
    ends = jnp.array([0, 4 * LENGTH - 1], dtype=jnp.int32)
    return jnp.sort(jnp.concatenate([ends, chosen])).astype(jnp.int32)


def block_levels(own_key, extent, shards, smallest, largest):
    def one(position, blocks):
        heights = jax.random.uniform(jax.random.fold_in(jax.random.fold_in(own_key, 6), position), (blocks,), jnp.float32, smallest / len(shards), largest / len(shards))
        return jnp.repeat(jnp.exp(heights), extent[position] // blocks).reshape((-1,) + (1,) * (len(extent) - position - 1))

    gain = one(*shards[0])
    for cut in shards[1:]:
        gain = gain * one(*cut)
    return gain


def bell_draw(own_key, extent, deviation, most, pieces=(), kind=jnp.bfloat16):
    gain = block_levels(own_key, extent, pieces, -0.22, 0.18) if pieces else 1.0
    values = jax.random.normal(own_key, extent, jnp.float32) * deviation * gain
    return jnp.minimum(jnp.maximum(values, -most), most).astype(kind)


def setup_inputs(seed: int = 0) -> dict:
    arg_keys = jax.random.split(jax.random.key(seed), 21)
    return {
        "pair_state": draw_pair_state(jax.random.fold_in(arg_keys[20], 71), 0),
        "seq_state": draw_seq_state(jax.random.fold_in(arg_keys[20], 71), 0),
        "residue_index": draw_residue_index(jax.random.fold_in(arg_keys[20], 71), 0),
        "residue_mask": draw_residue_mask(jax.random.fold_in(arg_keys[20], 71), 0),
        "position_table": bell_draw(arg_keys[4], (RELPOS_BINS, CZ), 1.0, 4.0),
        "attention_gain": jnp.clip(1.0 + 0.18 * jax.random.normal(arg_keys[5], (LAYERS, CS), jnp.float32), 0.1, 1.9),
        "bias_norm_gain": jnp.clip(1.0 + 0.18 * jax.random.normal(arg_keys[6], (LAYERS, CZ), jnp.float32), 0.1, 1.9),
        "query_weight": draw_query_weight(jax.random.fold_in(arg_keys[20], 71), 0),
        "key_weight": draw_key_weight(jax.random.fold_in(arg_keys[20], 71), 0),
        "value_weight": bell_draw(arg_keys[9], (LAYERS, CS, CS), CS ** -0.5, 0.1875, ((2, 8),)),
        "gate_weight": bell_draw(arg_keys[10], (LAYERS, CS, CS), CS ** -0.5, 0.1875, ((2, 8),)),
        "out_weight": bell_draw(arg_keys[11], (LAYERS, CS, CS), (CS // 16) ** -0.5, 0.75, ((2, 8),)),
        "bias_weight": bell_draw(arg_keys[12], (LAYERS, CZ, HEADS), (CZ // 9) ** -0.5, 1.5),
        "outer_gain": jnp.clip(1.0 + 0.18 * jax.random.normal(arg_keys[13], (LAYERS, CS), jnp.float32), 0.1, 1.9),
        "outer_weight": bell_draw(arg_keys[14], (LAYERS, CS, 2 * INNER), CS ** -0.5, 0.1875),
        "outer_out_weight": bell_draw(arg_keys[15], (LAYERS, 2 * INNER, CZ), (2 * INNER) ** -0.5, 0.5),
        "transition_gain": jnp.clip(1.0 + 0.18 * jax.random.normal(arg_keys[16], (LAYERS, CZ), jnp.float32), 0.1, 1.9),
        "up_weight": bell_draw(arg_keys[17], (LAYERS, CZ, FFZ), CZ ** -0.5, 0.5),
        "down_weight": bell_draw(arg_keys[18], (LAYERS, FFZ, CZ), FFZ ** -0.5, 0.25),
        "distance_weight": bell_draw(arg_keys[19], (CZ, BINS), CZ ** -0.5, 0.5),
    }


def normalize(values, weight_gain):
    average = lax.optimization_barrier(jnp.mean(values, axis=-1, keepdims=True))
    centred = values - average
    spread = lax.optimization_barrier(jnp.mean(centred * centred, axis=-1, keepdims=True))
    return centred * lax.rsqrt(spread + 1e-05) * weight_gain.astype(jnp.float32)

def settle(values):
    rounded = lax.optimization_barrier(values.astype(jnp.bfloat16))
    return rounded.astype(jnp.float32)

def reference(pair_state, seq_state, residue_index, residue_mask, position_table, attention_gain, bias_norm_gain, query_weight, key_weight, value_weight, gate_weight, out_weight, bias_weight, outer_gain, outer_weight, outer_out_weight, transition_gain, up_weight, down_weight, distance_weight):
    length = seq_state.shape[0]
    blocks = N_ROW
    block_rows = length // blocks
    live_mask = residue_mask > 0
    pair_live = live_mask[:, None] & live_mask[None, :]
    offset = jnp.clip(residue_index[None, :] - residue_index[:, None], -RELPOS_MAX, RELPOS_MAX) + RELPOS_MAX + 1
    bin_index = jnp.where(pair_live, offset, 0).astype(jnp.int32)
    pair_now = pair_state.astype(jnp.float32) + position_table.astype(jnp.float32)[bin_index]
    seq_now = seq_state
    score_scale = HEAD_DIM ** (-0.5)
    for layer_index in range(LAYERS):
        normed_seq = normalize(seq_now.astype(jnp.float32), attention_gain[layer_index]).astype(jnp.bfloat16)
        queries = (jnp.dot(normed_seq, query_weight[layer_index], preferred_element_type=jnp.float32) * score_scale).astype(jnp.bfloat16)
        keys_local = jnp.dot(normed_seq, key_weight[layer_index], preferred_element_type=jnp.float32).astype(jnp.bfloat16)
        values_local = jnp.dot(normed_seq, value_weight[layer_index], preferred_element_type=jnp.float32).astype(jnp.bfloat16)
        gating = jax.nn.sigmoid(jnp.dot(normed_seq, gate_weight[layer_index], preferred_element_type=jnp.float32))

        def bias_block(pair_tile):
            normed_pair = normalize(pair_tile, bias_norm_gain[layer_index]).astype(jnp.bfloat16)
            return jnp.einsum('ijc,ch->hij', normed_pair.astype(jnp.float32), bias_weight[layer_index].astype(jnp.float32)).astype(jnp.bfloat16)
        pair_bias = lax.map(bias_block, pair_now.reshape(blocks, block_rows, length, CZ))
        pair_bias = jnp.transpose(pair_bias, (1, 0, 2, 3)).reshape(HEADS, length, length)
        head_query = jnp.transpose(queries.reshape(length, HEADS, HEAD_DIM), (1, 0, 2))
        head_key = jnp.transpose(keys_local.reshape(length, HEADS, HEAD_DIM), (1, 0, 2))
        head_value = jnp.transpose(values_local.reshape(length, HEADS, HEAD_DIM), (1, 0, 2))

        def attend(inputs):
            one_query, one_key, one_value, one_bias = inputs
            scores = jnp.dot(one_query, one_key.T, preferred_element_type=jnp.float32) + one_bias.astype(jnp.float32)
            scores = jnp.where(live_mask[None, :], scores, -jnp.inf)
            row_max = lax.optimization_barrier(jnp.max(scores, axis=-1, keepdims=True))
            shifted = jnp.exp(scores - row_max)
            weights = (shifted / lax.optimization_barrier(jnp.sum(shifted, axis=-1, keepdims=True))).astype(jnp.bfloat16)
            return jnp.dot(weights, one_value, preferred_element_type=jnp.float32)
        attended = lax.map(attend, (head_query, head_key, head_value, pair_bias))
        attended = jnp.transpose(attended, (1, 0, 2)).reshape(length, CS)
        gated_out = (gating * attended).astype(jnp.bfloat16)
        seq_now = (seq_now.astype(jnp.float32) + jnp.dot(gated_out, out_weight[layer_index], preferred_element_type=jnp.float32)).astype(jnp.bfloat16)
        outer_in = normalize(seq_now.astype(jnp.float32), outer_gain[layer_index]).astype(jnp.bfloat16)
        projected = jnp.dot(outer_in, outer_weight[layer_index], preferred_element_type=jnp.float32)
        left_side = projected[:, :INNER].astype(jnp.bfloat16)
        right_wide = projected[:, INNER:].astype(jnp.bfloat16).astype(jnp.float32)[None, :, :]

        def pair_block(inputs):
            pair_tile, left_rows = inputs
            left_wide = left_rows.astype(jnp.float32)[:, None, :]
            features = jnp.concatenate([left_wide * right_wide, left_wide - right_wide], axis=-1).astype(jnp.bfloat16)
            pair_mid = pair_tile + jnp.dot(features.reshape(-1, 2 * INNER), outer_out_weight[layer_index], preferred_element_type=jnp.float32).reshape(pair_tile.shape)
            normed_pair = normalize(pair_mid, transition_gain[layer_index]).astype(jnp.bfloat16)
            hidden = jax.nn.relu(jnp.dot(normed_pair.reshape(-1, CZ), up_weight[layer_index], preferred_element_type=jnp.float32)).astype(jnp.bfloat16)
            return settle(pair_mid + jnp.dot(hidden, down_weight[layer_index], preferred_element_type=jnp.float32).reshape(pair_tile.shape))
        pair_now = lax.map(pair_block, (pair_now.reshape(blocks, block_rows, length, CZ), left_side.reshape(blocks, block_rows, INNER))).reshape(length, length, CZ)
    final_pair = pair_now.astype(jnp.bfloat16)

    def logit_block(pair_tile):
        return jnp.dot(pair_tile.reshape(-1, CZ), distance_weight, preferred_element_type=jnp.float32).astype(jnp.bfloat16).reshape(pair_tile.shape[0], length, BINS)
    logits = lax.map(logit_block, final_pair.reshape(blocks, block_rows, length, CZ)).reshape(length, length, BINS)
    mirrored = jnp.transpose(logits, (1, 0, 2))
    distogram = ((logits.astype(jnp.float32) + mirrored.astype(jnp.float32)) * 0.5).astype(jnp.bfloat16)
    return (distogram, seq_now)
```

```python
import jax
import jax.numpy as jnp
from jax import lax
from jax.experimental import pallas as pl
from jax.experimental.pallas import tpu as pltpu
from jax.sharding import PartitionSpec as P

HEAD_DIM = 32
RELPOS_MAX = 32
MESH = pl.DeviceIdType.MESH
OWN = 16


def normalize(values, weight_gain):
    average = jnp.mean(values, axis=-1, keepdims=True)
    centred = values - average
    spread = jnp.mean(centred * centred, axis=-1, keepdims=True)
    return centred * lax.rsqrt(spread + 1e-05) * weight_gain


def full_spec():
    return pl.BlockSpec(memory_space=pltpu.VMEM)


def any_spec():
    return pl.BlockSpec(memory_space=pl.ANY)


def remote(source, target, send, recv, where):
    return pltpu.make_async_remote_copy(
        src_ref=source,
        dst_ref=target,
        send_sem=send,
        recv_sem=recv,
        device_id=where,
        device_id_type=MESH,
    )


def settle(ref, sem):
    pltpu.make_async_copy(ref, ref, sem).wait()


def rows_at(start, size, step):
    return pl.ds(pl.multiple_of(start, step), size)


def trunk(pair_state, seq_tile, index_row, mask_row, table, gains, bias_weight_t, dist_t, mats):
    nr, nc = lax.axis_size("row"), lax.axis_size("col")
    tr, tc, ch = pair_state.shape
    width = seq_tile.shape[1]
    layers, cs = mats[0].shape[:2]
    heads = bias_weight_t.shape[1]
    hl = heads // nc
    length = nr * tr
    lanes = (tr + 127) // 128 * 128
    owners, per, parts = tr // OWN, tc // OWN, tr // tc
    chunks, half = tc // OWN, OWN // 2
    wide = mats[5].shape[2]
    bins = dist_t.shape[0]
    packed_rows = half * tc
    depth = packed_rows // nc
    score_scale = HEAD_DIM ** (-0.5)
    f32, bf16 = jnp.float32, jnp.bfloat16

    def kernel(*refs):
        it = iter(refs)
        pair_hbm, seq_ref, index_ref, mask_ref, table_ref = (next(it) for _ in range(5))
        att_gain, bias_gain, outer_gain, trans_gain = (next(it) for _ in range(4))
        bias_w, dist_ref = (next(it) for _ in range(2))
        q_hbm, k_hbm, v_hbm, g_hbm, out_hbm = (next(it) for _ in range(5))
        late_hbm = [next(it) for _ in range(4)]
        final_ref, seq_out = (next(it) for _ in range(2))
        q_w, k_w, v_w, g_w = (next(it) for _ in range(4))
        late_refs = [next(it) for _ in range(4)]
        outer_w, mix_w, up_w, down_w = late_refs
        pair_in, natural, pair_s, mixed, place, table_s, bins_s = (next(it) for _ in range(7))
        gathered, kv_all, bias_out, bias_all, query_s, gate_s = (next(it) for _ in range(6))
        wrow, stage, rs_recv, new_rows, lr_s, left_all, right_all = (next(it) for _ in range(7))
        left_dup, right_rep, seq_next, out_stage = (next(it) for _ in range(4))
        fresh_s, own_s, flat, spread_s, moved, landed, unpacked = (next(it) for _ in range(7))
        load_sem, seq_sem, w_sem, bias_send, bias_recv, kv_sem = (next(it) for _ in range(6))
        rs_sem, left_sem, right_sem, next_sem, out_sem = (next(it) for _ in range(5))
        one_sem, two_sem, three_sem = (next(it) for _ in range(3))

        row, col = lax.axis_index("row"), lax.axis_index("col")
        owner = jnp.minimum(col, owners - 1)
        holder, part_at = lax.div(col, parts), lax.rem(col, parts)

        pair_load = pltpu.make_async_copy(pair_hbm, pair_in, load_sem.at[0])
        pair_load.start()
        loads = [
            pltpu.make_async_copy(src, dst, load_sem.at[1 + n])
            for n, (src, dst) in enumerate(
                zip([k_hbm, v_hbm, q_hbm, g_hbm, *late_hbm], [k_w, v_w, q_w, g_w, *late_refs])
            )
        ]
        for load in loads:
            load.start()

        barrier = pltpu.get_barrier_semaphore()
        for step in range(1, nc):
            pl.semaphore_signal(
                barrier, inc=1, device_id={"col": lax.rem(col + step, nc)}, device_id_type=MESH
            )
        for step in range(1, nr):
            pl.semaphore_signal(
                barrier, inc=1, device_id={"row": lax.rem(row + step, nr)}, device_id_type=MESH
            )

        @pl.when(row != holder)
        def _():
            for slot in range(per):
                pl.semaphore_signal(
                    barrier,
                    inc=1,
                    device_id={"row": holder, "col": part_at * per + slot},
                    device_id_type=MESH,
                )

        is_owner = col < owners

        @pl.when(is_owner)
        def _():
            pl.semaphore_wait(barrier, nc + 2 * nr - 3)

        @pl.when(jnp.logical_not(is_owner))
        def _():
            pl.semaphore_wait(barrier, nc + nr - 2)

        for step in range(1, nc):
            remote(
                seq_ref,
                gathered.at[col],
                seq_sem.at[0],
                seq_sem.at[1],
                {"col": lax.rem(col + step, nc)},
            ).start()
        gathered[col] = seq_ref[...]
        for step in range(1, nc):
            peer = lax.rem(col + step, nc)
            remote(
                out_hbm.at[:, rows_at(peer * width, width, width), :],
                wrow.at[col],
                w_sem.at[0],
                w_sem.at[1],
                {"col": peer},
            ).start()
        own_w = pltpu.make_async_copy(
            out_hbm.at[:, rows_at(col * width, width, width), :], wrow.at[col], w_sem.at[2]
        )
        own_w.start()

        coded = jnp.where(mask_ref[...] > 0, index_ref[...], -1).astype(f32)
        for block in range(length // 128):
            line = coded[:, block * 128 : (block + 1) * 128]
            place[block * 128 : (block + 1) * 128, :] = jnp.broadcast_to(line, (128, 128)).T
        table_s[...] = jnp.zeros_like(table_s)
        table_s[0 : table_ref.shape[0], :] = table_ref[...].astype(f32)
        table_rows = table_s[...].astype(bf16)
        bins_s[...] = jnp.zeros_like(bins_s)
        bins_s[0:bins, 0:ch] = dist_ref[...]
        bins_s[bins : 2 * bins, ch : 2 * ch] = dist_ref[...]
        lane = lax.broadcasted_iota(jnp.int32, (1, ch), 1).astype(f32)
        low = lax.broadcasted_iota(jnp.int32, (1, ch), 1) < ch // 2

        def bias_of(layer, normed, at):
            mixed[pl.ds(pl.multiple_of(at * heads, heads), heads), 0:tr] = lax.dot_general(
                bias_w[layer], normed, (((1,), (1,)), ((), ())), preferred_element_type=f32
            )

        def send_bias(layer, k):
            span = pl.ds(k * OWN, OWN)
            for head in range(heads):
                bias_out[layer, head, k * OWN : (k + 1) * OWN, :] = mixed[
                    pl.ds(head, OWN, stride=heads), :
                ].astype(bf16)
            for step in range(1, nc):
                peer = lax.rem(col + step, nc)
                remote(
                    bias_out.at[layer, pl.ds(peer * hl, hl), span],
                    bias_all.at[layer, col, :, span],
                    bias_send.at[layer, k],
                    bias_recv.at[layer, k],
                    {"col": peer},
                ).start()
            bias_all[layer, col, :, k * OWN : (k + 1) * OWN, :] = bias_out[
                layer, pl.ds(col * hl, hl), k * OWN : (k + 1) * OWN, :
            ]

        def enter(k):
            natural[...] = (
                pair_in[:, k * OWN : (k + 1) * OWN, :].reshape(tr * OWN, ch).astype(f32)
            )

            @pl.loop(0, OWN, unroll=8)
            def _(j):
                row_pos = place[rows_at(row * tr, tr, 8), :]
                col_pos = place[pl.ds(col * tc + k * OWN + j, 1), :]
                offset = jnp.clip(col_pos - row_pos, -RELPOS_MAX, RELPOS_MAX) + (RELPOS_MAX + 1)
                live = (row_pos >= 0) & (col_pos >= 0)
                position = jnp.where(live, offset, 0.0)
                one_hot = jnp.where(position == lane, 1.0, 0.0).astype(bf16)
                value = natural[pl.ds(j, tr, stride=OWN), :] + jnp.dot(
                    one_hot, table_rows, preferred_element_type=f32
                )
                pair_s[rows_at((k * OWN + j) * tr, tr, 8), :] = value
                bias_of(0, normalize(value, bias_gain[0:1, :]).astype(bf16), j)

            send_bias(0, k)

        def project(layer, entering):
            normed = normalize(entering, att_gain[layer : layer + 1, :]).astype(bf16)

            def product(weight):
                return jnp.dot(normed, weight[layer], preferred_element_type=f32)

            if layer == 0:
                loads[0].wait()
            kv_all[layer, row, 0] = product(k_w).astype(bf16)
            if layer == 0:
                loads[1].wait()
            kv_all[layer, row, 1] = product(v_w).astype(bf16)
            for step in range(1, nr):
                remote(
                    kv_all.at[layer, row],
                    kv_all.at[layer, row],
                    kv_sem.at[layer, 0],
                    kv_sem.at[layer, 1],
                    {"row": lax.rem(row + step, nr)},
                ).start()
            if layer == 0:
                loads[2].wait()
            query_s[...] = (product(q_w) * score_scale).astype(bf16)
            if layer == 0:
                loads[3].wait()
            gate_s[...] = jax.nn.sigmoid(product(g_w))

        def attend(layer):
            settle(kv_all.at[layer, pl.ds(0, nr - 1)], kv_sem.at[layer, 1])
            for k in range(chunks):
                settle(
                    bias_all.at[layer, pl.ds(0, nc - 1), :, pl.ds(k * OWN, OWN)],
                    bias_recv.at[layer, k],
                )
            keys = kv_all[layer, :, 0].reshape(length, width)
            values = kv_all[layer, :, 1].reshape(length, width)
            live = place[:, 0:tr] >= 0
            head_of = lax.broadcasted_iota(jnp.int32, (tr, width), 1) // HEAD_DIM
            queries = query_s[...].astype(f32)
            attended = jnp.zeros((tr, width), f32)
            for head in range(hl):
                own = head_of == head
                query = jnp.where(own, queries, 0.0).astype(bf16)
                scores = lax.dot_general(
                    keys, query, (((1,), (1,)), ((), ())), preferred_element_type=f32
                )
                bias = bias_all[layer, :, head].reshape(length, lanes)[:, :tr]
                scores = jnp.where(live, scores + bias.astype(f32), -jnp.inf)
                shifted = jnp.exp(scores - jnp.max(scores, axis=0, keepdims=True))
                share = (shifted / jnp.sum(shifted, axis=0, keepdims=True)).astype(bf16)
                mixture = lax.dot_general(
                    share, values, (((0,), (0,)), ((), ())), preferred_element_type=f32
                )
                attended = jnp.where(own, mixture, attended)
            gated = (gate_s[...] * attended).astype(bf16)
            if layer == 0:
                own_w.wait()
                settle(wrow.at[pl.ds(0, nc - 1)], w_sem.at[1])
            weight = jnp.concatenate([wrow[p, layer] for p in range(nc)], axis=1)
            partial = jnp.dot(gated, weight, preferred_element_type=f32)
            stage[layer] = partial.reshape(owners, OWN, cs).astype(bf16)
            for step in range(owners):
                peer = lax.rem(col + step, owners)

                @pl.when(peer != col)
                def _(peer=peer):
                    remote(
                        stage.at[layer, peer],
                        rs_recv.at[layer, col],
                        rs_sem.at[layer, 0],
                        rs_sem.at[layer, 1],
                        {"col": peer},
                    ).start()

        def finish_rows(layer):
            at = rows_at(owner * OWN, OWN, OWN)

            @pl.when(is_owner)
            def _():
                rs_recv[layer, col] = stage[layer, owner]
                if layer == 0:
                    before = jnp.concatenate([gathered[p, at, :] for p in range(nc)], axis=1)
                else:
                    before = seq_next[at, :]
                total = before.astype(f32)
                settle(rs_recv.at[layer, pl.ds(0, nc - 1)], rs_sem.at[layer, 1])
                for p in range(nc):
                    total += rs_recv[layer, p].astype(f32)
                fresh = total.astype(bf16)
                new_rows[layer] = fresh
                outer_in = normalize(fresh.astype(f32), outer_gain[layer : layer + 1, :])
                lr_s[layer] = jnp.dot(
                    outer_in.astype(bf16), outer_w[layer], preferred_element_type=f32
                ).astype(bf16)
                slot = rows_at(lax.rem(owner, per) * OWN, OWN, OWN)
                for step in range(1, nr):
                    remote(
                        lr_s.at[layer],
                        right_all.at[layer, slot],
                        right_sem.at[layer, 0],
                        right_sem.at[layer, 1],
                        {
                            "row": lax.rem(row + step, nr),
                            "col": parts * row + lax.div(owner, per),
                        },
                    ).start()
                for step in range(1, nc):
                    remote(
                        lr_s.at[layer],
                        left_all.at[layer, at],
                        left_sem.at[layer, 0],
                        left_sem.at[layer, 1],
                        {"col": lax.rem(col + step, nc)},
                    ).start()
                left_all[layer, at, :] = lr_s[layer]
                if layer < layers - 1:
                    for step in range(1, nc):
                        remote(
                            new_rows.at[layer],
                            seq_next.at[at],
                            next_sem.at[0],
                            next_sem.at[1],
                            {"col": lax.rem(col + step, nc)},
                        ).start()
                    seq_next[at, :] = fresh
                else:
                    for p in range(nc):
                        out_stage[p] = fresh[:, p * width : (p + 1) * width]
                    for step in range(1, nc):
                        peer = lax.rem(col + step, nc)
                        remote(
                            out_stage.at[peer],
                            seq_out.at[at],
                            out_sem.at[0],
                            out_sem.at[1],
                            {"col": peer},
                        ).start()
                    seq_out[at, :] = out_stage[col]

        def from_owners(whole, most, sem):
            pl.when(is_owner)(lambda: settle(most, sem))
            pl.when(jnp.logical_not(is_owner))(lambda: settle(whole, sem))

        some = pl.ds(0, (owners - 1) * OWN)

        def sides(layer):
            from_owners(left_all.at[layer], left_all.at[layer, some], left_sem.at[layer, 1])

            @pl.when(row != holder)
            def _():
                settle(right_all.at[layer], right_sem.at[layer, 1])

            @pl.when(row == holder)
            def _():
                right_all[layer] = left_all[layer, rows_at(part_at * tc, tc, OWN), :]

            left = left_all[layer].astype(f32)
            left_dup[...] = jnp.where(low, left, pltpu.roll(left, ch // 2, axis=1))
            right = right_all[layer].astype(f32)
            right = jnp.where(low, pltpu.roll(right, ch // 2, axis=1), right)
            right_rep[...] = jnp.broadcast_to(right[:, None, :], (tc, 8, ch))

        group = 4

        def update(layer, k):
            last = layer == layers - 1
            trans = trans_gain[layer : layer + 1, :]

            @pl.loop(0, OWN // group, unroll=2)
            def _(step):
                j = pl.multiple_of(step * group, group) + k * OWN
                at = rows_at(j * tr, group * tr, 8)
                right = right_rep[pl.ds(j, group)][:, None]
                left = left_dup[...].reshape(1, tr // 8, 8, ch)
                features = jnp.where(low.reshape(1, 1, 1, ch), left * right, left - right)
                features = features.reshape(group * tr, ch).astype(bf16)
                middle = pair_s[at, :] + jnp.dot(
                    features, mix_w[layer], preferred_element_type=f32
                )
                normed = normalize(middle, trans).astype(bf16)
                hidden = jnp.maximum(
                    jnp.dot(normed, up_w[layer], preferred_element_type=f32), 0.0
                ).astype(bf16)
                fresh = (
                    middle + jnp.dot(hidden, down_w[layer], preferred_element_type=f32)
                ).astype(bf16)
                if last:
                    fresh_s[pl.ds(step * group, group)] = fresh.reshape(group, parts, tc, ch)
                else:
                    value = fresh.astype(f32)
                    pair_s[at, :] = value
                    normed = normalize(value, bias_gain[layer + 1 : layer + 2, :]).astype(bf16)
                    for n in range(group):
                        bias_of(layer + 1, normed[n * tr : (n + 1) * tr], step * group + n)

        def logits(k):
            for s in range(parts):
                both = jnp.concatenate(
                    [
                        fresh_s[0:half, s].reshape(packed_rows, ch),
                        fresh_s[half:OWN, s].reshape(packed_rows, ch),
                    ],
                    axis=1,
                )
                packed = lax.dot_general(
                    both, bins_s[...], (((1,), (1,)), ((), ())), preferred_element_type=f32
                )
                own_s[k, s] = packed
                rounded = packed.astype(bf16)
                for p in range(nc):
                    flat[k, p, s] = rounded[p * depth : (p + 1) * depth]
            for step in range(1, nc):
                peer = lax.rem(col + step, nc)
                remote(
                    flat.at[k, peer],
                    spread_s.at[k, col],
                    one_sem.at[k, 0],
                    one_sem.at[k, 1],
                    {"col": peer},
                ).start()

        def across(k):
            settle(spread_s.at[k, pl.ds(0, nc - 1)], one_sem.at[k, 1])
            for step in range(nc):
                origin = lax.rem(col + step, nc)
                peer, slot = lax.div(origin, parts), lax.rem(origin, parts)
                source = spread_s.at[k, origin] if step else flat.at[k, col]
                target = moved.at[k, row, slot]

                @pl.when(peer != row)
                def _(source=source, target=target, peer=peer):
                    remote(
                        source, target, two_sem.at[k, 0], two_sem.at[k, 1], {"row": peer}
                    ).start()

                @pl.when(peer == row)
                def _(source=source, target=target):
                    pltpu.make_async_copy(source, target, two_sem.at[k, 1]).start()

        def home(k):
            settle(moved.at[k], two_sem.at[k, 1])
            for step in range(nr):
                origin = lax.rem(row + step, nr)
                for s in range(parts):
                    peer = origin * parts + s
                    for slot in range(parts):
                        source = moved.at[k, origin, slot, s]
                        target = landed.at[k, slot, col]

                        @pl.when(peer != col)
                        def _(source=source, target=target, peer=peer):
                            remote(
                                source,
                                target,
                                three_sem.at[k, 0],
                                three_sem.at[k, 1],
                                {"col": peer},
                            ).start()

                        @pl.when(peer == col)
                        def _(source=source, target=target):
                            pltpu.make_async_copy(source, target, three_sem.at[k, 1]).start()

        def combine(k):
            settle(landed.at[k], three_sem.at[k, 1])
            for slot in range(parts):
                for p in range(nc):
                    unpacked[slot, p * depth : (p + 1) * depth, :] = landed[k, slot, p].astype(f32)

                @pl.loop(0, half, unroll=4)
                def _(n, slot=slot):
                    near = unpacked[slot, rows_at(n * tc, tc, 8), :]
                    far = pltpu.roll(near, bins, axis=1)
                    for other, at in ((near, n), (far, n + half)):
                        at = at + k * OWN
                        pieces = []
                        for c in range(chunks):
                            own = own_s[c, slot, pl.ds(at, half, stride=tc), :]
                            pieces += [own, pltpu.roll(own, bins, axis=1)]
                        total = (jnp.concatenate(pieces, axis=0) + other) * 0.5
                        final_ref[slot * tc + at] = total.astype(bf16)[:, :bins]

        pair_load.wait()
        for k in range(chunks):
            enter(k)
        settle(gathered.at[pl.ds(0, nc - 1)], seq_sem.at[1])
        project(0, jnp.concatenate([gathered[p] for p in range(nc)], axis=1).astype(f32))
        for layer in range(layers):
            attend(layer)
            if layer == 0:
                for load in loads[4:]:
                    load.wait()
            finish_rows(layer)
            sides(layer)
            if layer < layers - 1:
                for k in range(chunks):
                    update(layer, k)
                    send_bias(layer + 1, k)
                    if k == 0:
                        from_owners(seq_next, seq_next.at[some], next_sem.at[1])
                        project(layer + 1, seq_next[...].astype(f32))
        for k in range(chunks):
            update(layers - 1, k)
            logits(k)
            if k >= 1:
                across(k - 1)
            if k >= 2:
                home(k - 2)
        across(chunks - 1)
        for k in range(max(chunks - 2, 0), chunks):
            home(k)
        for k in range(chunks):
            combine(k)
        from_owners(seq_out, seq_out.at[some], out_sem.at[1])

        settle(gathered.at[pl.ds(0, nc - 1)], seq_sem.at[0])
        settle(wrow.at[pl.ds(0, nc - 1)], w_sem.at[0])
        for layer in range(layers):
            for k in range(chunks):
                settle(
                    bias_out.at[layer, pl.ds(0, (nc - 1) * hl), pl.ds(k * OWN, OWN)],
                    bias_send.at[layer, k],
                )
            settle(kv_all.at[layer, pl.ds(0, nr - 1)], kv_sem.at[layer, 0])

            from_owners(
                stage.at[layer], stage.at[layer, pl.ds(0, owners - 1)], rs_sem.at[layer, 0]
            )

            @pl.when(is_owner)
            def _(layer=layer):
                settle(
                    rs_recv.at[layer, pl.ds(0, nr - 1), :, pl.ds(0, wide)],
                    right_sem.at[layer, 0],
                )
                settle(
                    rs_recv.at[layer, pl.ds(0, nc - 1), :, pl.ds(0, wide)],
                    left_sem.at[layer, 0],
                )
                if layer < layers - 1:
                    settle(rs_recv.at[layer, pl.ds(0, nc - 1)], next_sem.at[0])
                else:
                    settle(out_stage.at[pl.ds(0, nc - 1)], out_sem.at[0])

        for k in range(chunks):
            settle(flat.at[k, pl.ds(0, nc - 1)], one_sem.at[k, 0])
            settle(flat.at[k, pl.ds(0, nc - parts)], two_sem.at[k, 0])
            settle(landed.at[k, :, pl.ds(0, nc - 1)], three_sem.at[k, 0])

    operands = (
        pair_state, seq_tile, index_row, mask_row, table, *gains, bias_weight_t, dist_t, *mats,
    )
    vm, dma = pltpu.VMEM, pltpu.SemaphoreType.DMA
    scratch = (
        [vm((layers, cs, width), bf16)] * 4
        + [vm(m.shape, bf16) for m in mats[5:]]
        + [
            vm((tr, tc, ch), bf16),
            vm((tr * OWN, ch), f32),
            vm((tc * tr, ch), f32),
            vm((OWN * heads, lanes), f32),
            vm((length, 128), f32),
            vm(((table.shape[0] + 127) // 128 * 128, ch), f32),
            vm((2 * bins, 2 * ch), bf16),
            vm((nc, tr, width), bf16),
            vm((layers, nr, 2, tr, width), bf16),
            vm((layers, heads, tc, lanes), bf16),
            vm((layers, nc, hl, tc, lanes), bf16),
            vm((tr, width), bf16),
            vm((tr, width), f32),
            vm((nc, layers, width, width), bf16),
            vm((layers, owners, OWN, cs), bf16),
            vm((layers, nc, OWN, cs), bf16),
            vm((layers, OWN, cs), bf16),
            vm((layers, OWN, wide), bf16),
            vm((layers, tr, wide), bf16),
            vm((layers, tc, wide), bf16),
            vm((tr, ch), f32),
            vm((tc, 8, ch), f32),
            vm((tr, cs), bf16),
            vm((nc, OWN, width), bf16),
            vm((OWN, parts, tc, ch), bf16),
            vm((chunks, parts, packed_rows, 2 * bins), f32),
            vm((chunks, nc, parts, depth, 2 * bins), bf16),
            vm((chunks, nc, parts, depth, 2 * bins), bf16),
            vm((chunks, nr, parts, parts, depth, 2 * bins), bf16),
            vm((chunks, parts, nc, depth, 2 * bins), bf16),
            vm((parts, packed_rows, 2 * bins), f32),
            dma((9,)),
            dma((2,)),
            dma((3,)),
            dma((layers, chunks)),
            dma((layers, chunks)),
            dma((layers, 2)),
            dma((layers, 2)),
            dma((layers, 2)),
            dma((layers, 2)),
            dma((2,)),
            dma((2,)),
            dma((chunks, 2)),
            dma((chunks, 2)),
            dma((chunks, 2)),
        ]
    )
    return pl.pallas_call(
        kernel,
        out_shape=(
            jax.ShapeDtypeStruct((tr, tc, bins), bf16),
            jax.ShapeDtypeStruct((tr, width), bf16),
        ),
        in_specs=[any_spec()] + [full_spec()] * 10 + [any_spec()] * 9,
        out_specs=(full_spec(),) * 2,
        scratch_shapes=scratch,
        compiler_params=pltpu.CompilerParams(collective_id=0, has_side_effects=True),
    )(*operands)


def per_device(
    pair_state,
    seq_state,
    residue_index,
    residue_mask,
    position_table,
    attention_gain,
    bias_norm_gain,
    query_weight,
    key_weight,
    value_weight,
    gate_weight,
    out_weight,
    bias_weight,
    outer_gain,
    outer_weight,
    outer_out_weight,
    transition_gain,
    up_weight,
    down_weight,
    distance_weight,
):
    return trunk(
        pair_state,
        seq_state,
        residue_index.reshape(1, -1),
        residue_mask.reshape(1, -1),
        position_table,
        (attention_gain, bias_norm_gain, outer_gain, transition_gain),
        jnp.swapaxes(bias_weight, 1, 2),
        distance_weight.T,
        (
            query_weight,
            key_weight,
            value_weight,
            gate_weight,
            out_weight,
            outer_weight,
            outer_out_weight,
            up_weight,
            down_weight,
        ),
    )


def solution(mesh):
    heads_split = P(None, None, "col")
    in_specs = (
        (P("row", "col", None), P("row", "col"))
        + (P(),) * 5
        + (heads_split,) * 5
        + (P(),) * 8
    )
    out_specs = (P("row", "col", None), P("row", "col"))
    return jax.shard_map(
        per_device, mesh=mesh, in_specs=in_specs, out_specs=out_specs, check_vma=False
    )
```

```python
import jax
import jax.numpy as jnp
from jax import lax
from jax.experimental import pallas as pl
from jax.experimental.pallas import tpu as pltpu
from jax.sharding import PartitionSpec as P

HEAD_DIM = 32
RELPOS_MAX = 32
MESH = pl.DeviceIdType.MESH
OWN = 16
PIECE = 8
FAR = 1e6


def normalize(values, weight_gain):
    average = jnp.mean(values, axis=-1, keepdims=True)
    centred = values - average
    spread = jnp.mean(centred * centred, axis=-1, keepdims=True)
    return centred * lax.rsqrt(spread + 1e-05) * weight_gain


def full_spec():
    return pl.BlockSpec(memory_space=pltpu.VMEM)


def any_spec():
    return pl.BlockSpec(memory_space=pl.ANY)


def remote(source, target, send, recv, where):
    return pltpu.make_async_remote_copy(
        src_ref=source,
        dst_ref=target,
        send_sem=send,
        recv_sem=recv,
        device_id=where,
        device_id_type=MESH,
    )


def settle(ref, sem):
    pltpu.make_async_copy(ref, ref, sem).wait()


def rows_at(start, size, step):
    return pl.ds(pl.multiple_of(start, step), size)


def trunk(pair_state, seq_tile, index, mask, table, gains, bias_weight_t, dist_t, mats):
    nr, nc = lax.axis_size("row"), lax.axis_size("col")
    tr, tc, ch = pair_state.shape
    width = seq_tile.shape[1]
    layers, cs = mats[0].shape[:2]
    heads = bias_weight_t.shape[1]
    hl = heads // nc
    length = nr * tr
    lanes = (tr + 127) // 128 * 128
    owners, per, parts = tr // OWN, tc // OWN, tr // tc
    chunks, spans, half = tc // OWN, tc // PIECE, tc // 2
    wide = mats[5].shape[2]
    bins = dist_t.shape[0]
    packed_rows = PIECE * half
    depth = packed_rows // nc
    score_scale = HEAD_DIM ** (-0.5)
    gap = OWN + 8
    f32, bf16 = jnp.float32, jnp.bfloat16

    def kernel(*refs):
        it = iter(refs)
        pair_hbm, seq_hbm = (next(it) for _ in range(2))
        small_hbm = [next(it) for _ in range(9)]
        q_hbm, k_hbm, v_hbm, g_hbm, out_hbm = (next(it) for _ in range(5))
        late_hbm = [next(it) for _ in range(4)]
        final_ref, seq_out = (next(it) for _ in range(2))
        small_refs = [next(it) for _ in range(9)]
        index_ref, mask_ref, table_ref = small_refs[:3]
        att_gain, bias_gain, outer_gain, trans_gain, bias_w, dist_ref = small_refs[3:]
        q_w, k_w, v_w, g_w = (next(it) for _ in range(4))
        late_refs = [next(it) for _ in range(4)]
        outer_w, mix_w, up_w, down_w = late_refs
        pair_in, natural, pair_s, mixed, place, table_s, bins_s = (next(it) for _ in range(7))
        home_w, mirror_s, score_s = (next(it) for _ in range(3))
        gathered, kv_all, bias_out, bias_all, query_s, gate_s, normed_s = (next(it) for _ in range(7))
        wrow, stage, rs_recv, new_rows, lr_s, left_all, right_all = (next(it) for _ in range(7))
        left_dup, right_rep, seq_next, out_stage = (next(it) for _ in range(4))
        flat, spread_s, moved, landed, unpacked = (next(it) for _ in range(5))
        load_sem, small_sem, seq_sem, w_sem, bias_send, bias_recv, kv_sem = (next(it) for _ in range(7))
        rs_sem, left_sem, right_sem, next_sem, out_sem = (next(it) for _ in range(5))
        one_sem, two_sem, three_sem = (next(it) for _ in range(3))

        row, col = lax.axis_index("row"), lax.axis_index("col")
        owner = jnp.minimum(col, owners - 1)
        holder, part_at = lax.div(col, parts), lax.rem(col, parts)

        barrier = pltpu.get_barrier_semaphore()
        for step in range(1, nc):
            pl.semaphore_signal(
                barrier, inc=1, device_id={"col": lax.rem(col + step, nc)}, device_id_type=MESH
            )
        for step in range(1, nr):
            pl.semaphore_signal(
                barrier, inc=1, device_id={"row": lax.rem(row + step, nr)}, device_id_type=MESH
            )

        @pl.when(row != holder)
        def _():
            for slot in range(per):
                pl.semaphore_signal(
                    barrier,
                    inc=1,
                    device_id={"row": holder, "col": part_at * per + slot},
                    device_id_type=MESH,
                )

        small = [
            pltpu.make_async_copy(src, dst, small_sem.at[n])
            for n, (src, dst) in enumerate(zip(small_hbm, small_refs))
        ]
        for load in small:
            load.start()
        pair_load = pltpu.make_async_copy(pair_hbm, pair_in, load_sem.at[0])
        pair_load.start()
        loads = [
            pltpu.make_async_copy(src, dst, load_sem.at[1 + n])
            for n, (src, dst) in enumerate(
                zip([k_hbm, v_hbm, q_hbm, g_hbm, *late_hbm], [k_w, v_w, q_w, g_w, *late_refs])
            )
        ]
        for load in loads:
            load.start()

        is_owner = col < owners

        @pl.when(is_owner)
        def _():
            pl.semaphore_wait(barrier, nc + 2 * nr - 3)

        @pl.when(jnp.logical_not(is_owner))
        def _():
            pl.semaphore_wait(barrier, nc + nr - 2)

        for step in range(1, nc):
            remote(
                seq_hbm,
                gathered.at[col],
                seq_sem.at[0],
                seq_sem.at[1],
                {"col": lax.rem(col + step, nc)},
            ).start()
        own_seq = pltpu.make_async_copy(seq_hbm, gathered.at[col], seq_sem.at[2])
        own_seq.start()
        own_w = pltpu.make_async_copy(
            out_hbm.at[:, rows_at(col * width, width, width), :], wrow.at[col], w_sem.at[2]
        )
        own_w.start()

        for load in small:
            load.wait()
        coded = jnp.where(mask_ref[...] > 0, index_ref[...].astype(f32), FAR).reshape(1, length)
        for block in range(length // 128):
            line = coded[:, block * 128 : (block + 1) * 128]
            place[block * 128 : (block + 1) * 128, :] = jnp.broadcast_to(line, (128, 128)).T
        table_s[...] = jnp.zeros_like(table_s)
        table_s[0 : table_ref.shape[0], :] = table_ref[...].astype(f32)
        table_rows = table_s[...].astype(bf16)
        bins_s[...] = jnp.zeros_like(bins_s)
        bins_s[0:bins, 0:ch] = dist_ref[...]
        bins_s[bins : 2 * bins, ch : 2 * ch] = dist_ref[...]
        home_w[...] = jnp.zeros_like(home_w)
        unit = lax.broadcasted_iota(jnp.int32, (bins, bins), 0) == lax.broadcasted_iota(
            jnp.int32, (bins, bins), 1
        )
        unit = jnp.where(unit, 1.0, 0.0).astype(bf16)
        for n in range(2):
            home_w[n, :, 0:ch] = dist_ref[...]
            home_w[n, :, ch + n * bins : ch + (n + 1) * bins] = unit
        lane = lax.broadcasted_iota(jnp.int32, (1, ch), 1).astype(f32)
        shift = lane - (RELPOS_MAX + 1)
        least = jnp.where(lane == 0, -4 * FAR, jnp.where(lane == 1, -FAR / 2, shift))
        most = jnp.where(lane == 0, -FAR / 2, jnp.where(lane == 2 * RELPOS_MAX + 1, FAR, shift))
        low = lax.broadcasted_iota(jnp.int32, (1, ch), 1) < ch // 2

        def bias_of(layer, normed, at):
            mixed[at * heads : (at + 1) * heads, 0:tr] = lax.dot_general(
                bias_w[layer], normed, (((1,), (1,)), ((), ())), preferred_element_type=f32
            )

        def send_bias(layer, k):
            span = pl.ds(k * OWN, OWN)
            for head in range(heads):
                bias_out[layer, head, k * OWN : (k + 1) * OWN, :] = mixed[
                    pl.ds(head, OWN, stride=heads), :
                ].astype(bf16)
            for step in range(1, nc):
                peer = lax.rem(col + step, nc)
                remote(
                    bias_out.at[layer, pl.ds(peer * hl, hl), span],
                    bias_all.at[layer, col, :, span],
                    bias_send.at[layer, k],
                    bias_recv.at[layer, k],
                    {"col": peer},
                ).start()
            bias_all[layer, col, :, k * OWN : (k + 1) * OWN, :] = bias_out[
                layer, pl.ds(col * hl, hl), k * OWN : (k + 1) * OWN, :
            ]

        def enter(k):
            for i in range(tr):
                natural[i * gap : i * gap + OWN, :] = pair_in[
                    i, k * OWN : (k + 1) * OWN, :
                ].astype(f32)

            row_pos = place[rows_at(row * tr, tr, 8), :]
            hots = []
            for j in range(OWN):
                col_pos = place[pl.ds(col * tc + k * OWN + j, 1), :]
                col_pos = jnp.where(col_pos < FAR, col_pos, -FAR)
                offset = col_pos - row_pos
                hot = (offset >= least) & (offset <= most)
                hots.append(jnp.where(hot, 1.0, 0.0).astype(bf16))
            value = jnp.concatenate(
                [natural[pl.ds(j, tr, stride=gap), :] for j in range(OWN)], axis=0
            ) + jnp.dot(jnp.concatenate(hots, axis=0), table_rows, preferred_element_type=f32)
            pair_s[k * OWN * tr : (k + 1) * OWN * tr, :] = value
            normed = normalize(value, bias_gain[0:1, :]).astype(bf16)
            for j in range(OWN):
                bias_of(0, normed[j * tr : (j + 1) * tr], j)
            send_bias(0, k)

        def swap_weights():
            for step in range(1, nc):
                peer = lax.rem(col + step, nc)
                remote(
                    out_hbm.at[:, rows_at(peer * width, width, width), :],
                    wrow.at[col],
                    w_sem.at[0],
                    w_sem.at[1],
                    {"col": peer},
                ).start()

        def product(layer, k, weight):
            if layer == 0:
                loads[k].wait()
            return jnp.dot(normed_s[...], weight[layer], preferred_element_type=f32)

        def project(layer, entering):
            normed_s[...] = normalize(entering, att_gain[layer : layer + 1, :]).astype(bf16)
            kv_all[layer, row, 0] = product(layer, 0, k_w).astype(bf16)
            kv_all[layer, row, 1] = product(layer, 1, v_w).astype(bf16)
            for step in range(1, nr):
                remote(
                    kv_all.at[layer, row],
                    kv_all.at[layer, row],
                    kv_sem.at[layer, 0],
                    kv_sem.at[layer, 1],
                    {"row": lax.rem(row + step, nr)},
                ).start()

        def project_rest(layer):
            query_s[...] = (product(layer, 2, q_w) * score_scale).astype(bf16)
            gate_s[...] = jax.nn.sigmoid(product(layer, 3, g_w))

        def attend(layer):
            settle(kv_all.at[layer, pl.ds(0, nr - 1)], kv_sem.at[layer, 1])
            keys = kv_all[layer, :, 0].reshape(length, width)
            values = kv_all[layer, :, 1].reshape(length, width)
            live = place[:, 0:tr] < FAR
            head_of = lax.broadcasted_iota(jnp.int32, (tr, width), 1) // HEAD_DIM
            queries = query_s[...].astype(f32)
            attended = jnp.zeros((tr, width), f32)
            for head in range(hl):
                query = jnp.where(head_of == head, queries, 0.0).astype(bf16)
                score_s[head, :, 0:tr] = lax.dot_general(
                    keys, query, (((1,), (1,)), ((), ())), preferred_element_type=f32
                )
            for k in range(chunks):
                settle(
                    bias_all.at[layer, pl.ds(0, nc - 1), :, pl.ds(k * OWN, OWN)],
                    bias_recv.at[layer, k],
                )
            for head in range(hl):
                own = head_of == head
                scores = score_s[head, :, 0:tr]
                bias = bias_all[layer, :, head].reshape(length, lanes)[:, :tr]
                scores = jnp.where(live, scores + bias.astype(f32), -jnp.inf)
                shifted = jnp.exp(scores - jnp.max(scores, axis=0, keepdims=True))
                share = (shifted * (1.0 / jnp.sum(shifted, axis=0, keepdims=True))).astype(bf16)
                mixture = lax.dot_general(
                    share, values, (((0,), (0,)), ((), ())), preferred_element_type=f32
                )
                attended = jnp.where(own, mixture, attended)
            gated = (gate_s[...] * attended).astype(bf16)
            if layer == 0:
                own_w.wait()
                settle(wrow.at[pl.ds(0, nc - 1)], w_sem.at[1])
            weight = jnp.concatenate([wrow[p, layer] for p in range(nc)], axis=1)
            partial = jnp.dot(gated, weight, preferred_element_type=f32)
            stage[layer] = partial.reshape(owners, OWN, cs).astype(bf16)
            for step in range(owners):
                peer = lax.rem(col + step, owners)

                @pl.when(peer != col)
                def _(peer=peer):
                    remote(
                        stage.at[layer, peer],
                        rs_recv.at[layer, col],
                        rs_sem.at[layer, 0],
                        rs_sem.at[layer, 1],
                        {"col": peer},
                    ).start()

        def finish_rows(layer):
            at = rows_at(owner * OWN, OWN, OWN)

            @pl.when(is_owner)
            def _():
                rs_recv[layer, col] = stage[layer, owner]
                if layer == 0:
                    before = jnp.concatenate([gathered[p, at, :] for p in range(nc)], axis=1)
                else:
                    before = seq_next[at, :]
                total = before.astype(f32)
                settle(rs_recv.at[layer, pl.ds(0, nc - 1)], rs_sem.at[layer, 1])
                for p in range(nc):
                    total += rs_recv[layer, p].astype(f32)
                fresh = total.astype(bf16)
                new_rows[layer] = fresh
                outer_in = normalize(fresh.astype(f32), outer_gain[layer : layer + 1, :])
                lr_s[layer] = jnp.dot(
                    outer_in.astype(bf16), outer_w[layer], preferred_element_type=f32
                ).astype(bf16)
                slot = rows_at(lax.rem(owner, per) * OWN, OWN, OWN)
                for step in range(1, nr):
                    remote(
                        lr_s.at[layer],
                        right_all.at[layer, slot],
                        right_sem.at[layer, 0],
                        right_sem.at[layer, 1],
                        {
                            "row": lax.rem(row + step, nr),
                            "col": parts * row + lax.div(owner, per),
                        },
                    ).start()
                for step in range(1, nc):
                    remote(
                        lr_s.at[layer],
                        left_all.at[layer, at],
                        left_sem.at[layer, 0],
                        left_sem.at[layer, 1],
                        {"col": lax.rem(col + step, nc)},
                    ).start()
                left_all[layer, at, :] = lr_s[layer]
                if layer < layers - 1:
                    for step in range(1, nc):
                        remote(
                            new_rows.at[layer],
                            seq_next.at[at],
                            next_sem.at[0],
                            next_sem.at[1],
                            {"col": lax.rem(col + step, nc)},
                        ).start()
                    seq_next[at, :] = fresh
                else:
                    for p in range(nc):
                        out_stage[p] = fresh[:, p * width : (p + 1) * width]
                    for step in range(1, nc):
                        peer = lax.rem(col + step, nc)
                        remote(
                            out_stage.at[peer],
                            seq_out.at[at],
                            out_sem.at[0],
                            out_sem.at[1],
                            {"col": peer},
                        ).start()
                    seq_out[at, :] = out_stage[col]

        def from_owners(whole, most, sem):
            pl.when(is_owner)(lambda: settle(most, sem))
            pl.when(jnp.logical_not(is_owner))(lambda: settle(whole, sem))

        some = pl.ds(0, (owners - 1) * OWN)

        def sides(layer):
            from_owners(left_all.at[layer], left_all.at[layer, some], left_sem.at[layer, 1])

            @pl.when(row != holder)
            def _():
                settle(right_all.at[layer], right_sem.at[layer, 1])

            @pl.when(row == holder)
            def _():
                right_all[layer] = left_all[layer, rows_at(part_at * tc, tc, OWN), :]

            left = left_all[layer].astype(f32)
            left_dup[...] = jnp.where(low, left, pltpu.roll(left, ch // 2, axis=1))
            right = right_all[layer].astype(f32)
            right = jnp.where(low, pltpu.roll(right, ch // 2, axis=1), right)
            right_rep[...] = jnp.broadcast_to(right[:, None, :], (tc, 8, ch))

        def update(layer, k, count):
            at = slice(k * count * tr, (k + 1) * count * tr)
            right = right_rep[k * count : (k + 1) * count][:, None]
            left = left_dup[...].reshape(1, tr // 8, 8, ch)
            features = jnp.where(low.reshape(1, 1, 1, ch), left * right, left - right)
            features = features.reshape(count * tr, ch).astype(bf16)
            middle = pair_s[at, :] + jnp.dot(features, mix_w[layer], preferred_element_type=f32)
            normed = normalize(middle, trans_gain[layer : layer + 1, :]).astype(bf16)
            hidden = jnp.maximum(
                jnp.dot(normed, up_w[layer], preferred_element_type=f32), 0.0
            ).astype(bf16)
            fresh = (
                middle + jnp.dot(hidden, down_w[layer], preferred_element_type=f32)
            ).astype(bf16)
            value = fresh.astype(f32)
            pair_s[at, :] = value
            if layer < layers - 1:
                normed = normalize(value, bias_gain[layer + 1 : layer + 2, :]).astype(bf16)
                for n in range(count):
                    bias_of(layer + 1, normed[n * tr : (n + 1) * tr], n)

        def logits(k):
            for s in range(parts):
                sides = [
                    jnp.concatenate(
                        [
                            pair_s[pl.ds((k * PIECE + j) * tr + s * tc + n * half, half), :]
                            for j in range(PIECE)
                        ],
                        axis=0,
                    )
                    for n in range(2)
                ]
                packed = lax.dot_general(
                    jnp.concatenate(sides, axis=1).astype(bf16),
                    bins_s[...],
                    (((1,), (1,)), ((), ())),
                    preferred_element_type=f32,
                ).astype(bf16)
                for p in range(nc):
                    flat[k, p, s] = packed[p * depth : (p + 1) * depth]
            for step in range(1, nc):
                peer = lax.rem(col + step, nc)
                remote(
                    flat.at[k, peer],
                    spread_s.at[k, col],
                    one_sem.at[k, 0],
                    one_sem.at[k, 1],
                    {"col": peer},
                ).start()

        def across(k):
            settle(spread_s.at[k, pl.ds(0, nc - 1)], one_sem.at[k, 1])
            for step in range(nc):
                origin = lax.rem(col + step, nc)
                peer, slot = lax.div(origin, parts), lax.rem(origin, parts)
                source = spread_s.at[k, origin] if step else flat.at[k, col]
                target = moved.at[k, row, slot]

                @pl.when(peer != row)
                def _(source=source, target=target, peer=peer):
                    remote(
                        source, target, two_sem.at[k, 0], two_sem.at[k, 1], {"row": peer}
                    ).start()

                @pl.when(peer == row)
                def _(source=source, target=target):
                    pltpu.make_async_copy(source, target, two_sem.at[k, 1]).start()

        def home(k):
            settle(moved.at[k], two_sem.at[k, 1])
            for step in range(nr):
                origin = lax.rem(row + step, nr)
                for s in range(parts):
                    peer = origin * parts + s
                    for slot in range(parts):
                        source = moved.at[k, origin, slot, s]
                        target = landed.at[k, slot, col]

                        @pl.when(peer != col)
                        def _(source=source, target=target, peer=peer):
                            remote(
                                source,
                                target,
                                three_sem.at[k, 0],
                                three_sem.at[k, 1],
                                {"col": peer},
                            ).start()

                        @pl.when(peer == col)
                        def _(source=source, target=target):
                            pltpu.make_async_copy(source, target, three_sem.at[k, 1]).start()

        def collect(k):
            settle(landed.at[k], three_sem.at[k, 1])
            for slot in range(parts):
                for p in range(nc):
                    unpacked[k % 2, slot, p * depth : (p + 1) * depth, :] = landed[
                        k, slot, p
                    ].astype(f32)

            @pl.loop(0, half, unroll=8)
            def _(n):
                for slot in range(parts):
                    start = slot * tc + k * PIECE
                    mirror_s[n, start : start + PIECE, :] = unpacked[
                        k % 2, slot, pl.ds(n, PIECE, stride=half), :
                    ]

        def combine():
            @pl.loop(0, half, unroll=4)
            def _(n):
                mirrored = mirror_s[n].astype(bf16)
                for side in range(2):
                    j = n + side * half
                    own = pair_s[rows_at(j * tr, tr, 8), :].astype(bf16)
                    total = lax.dot_general(
                        home_w[side],
                        jnp.concatenate([own, mirrored], axis=1),
                        (((1,), (1,)), ((), ())),
                        preferred_element_type=f32,
                    )
                    final_ref[j] = (total * 0.5).astype(bf16)

        pair_load.wait()
        enter(0)
        own_seq.wait()
        settle(gathered.at[pl.ds(0, nc - 1)], seq_sem.at[1])
        project(0, jnp.concatenate([gathered[p] for p in range(nc)], axis=1).astype(f32))
        swap_weights()
        for k in range(1, chunks):
            enter(k)
        project_rest(0)
        for layer in range(layers):
            attend(layer)
            if layer == 0:
                for load in loads[4:]:
                    load.wait()
            finish_rows(layer)
            sides(layer)
            if layer < layers - 1:
                for k in range(chunks):
                    update(layer, k, OWN)
                    send_bias(layer + 1, k)
                    if k == 0:
                        from_owners(seq_next, seq_next.at[some], next_sem.at[1])
                        project(layer + 1, seq_next[...].astype(f32))
                project_rest(layer + 1)
        for k in range(spans):
            update(layers - 1, k, PIECE)
            logits(k)
            if k >= 1:
                across(k - 1)
            if k >= 3:
                home(k - 3)
            if k >= 5:
                collect(k - 5)
        across(spans - 1)
        for k in range(max(spans - 3, 0), spans):
            home(k)
            if k >= 2:
                collect(k - 2)
        for k in range(max(spans - 2, 0), spans):
            collect(k)
        combine()
        from_owners(seq_out, seq_out.at[some], out_sem.at[1])

        settle(gathered.at[pl.ds(0, nc - 1)], seq_sem.at[0])
        settle(wrow.at[pl.ds(0, nc - 1)], w_sem.at[0])
        for layer in range(layers):
            for k in range(chunks):
                settle(
                    bias_out.at[layer, pl.ds(0, (nc - 1) * hl), pl.ds(k * OWN, OWN)],
                    bias_send.at[layer, k],
                )
            settle(kv_all.at[layer, pl.ds(0, nr - 1)], kv_sem.at[layer, 0])

            from_owners(
                stage.at[layer], stage.at[layer, pl.ds(0, owners - 1)], rs_sem.at[layer, 0]
            )

            @pl.when(is_owner)
            def _(layer=layer):
                settle(
                    rs_recv.at[layer, pl.ds(0, nr - 1), :, pl.ds(0, wide)],
                    right_sem.at[layer, 0],
                )
                settle(
                    rs_recv.at[layer, pl.ds(0, nc - 1), :, pl.ds(0, wide)],
                    left_sem.at[layer, 0],
                )
                if layer < layers - 1:
                    settle(rs_recv.at[layer, pl.ds(0, nc - 1)], next_sem.at[0])
                else:
                    settle(out_stage.at[pl.ds(0, nc - 1)], out_sem.at[0])

        for k in range(spans):
            settle(flat.at[k, pl.ds(0, nc - 1)], one_sem.at[k, 0])
            settle(flat.at[k, pl.ds(0, nc - parts)], two_sem.at[k, 0])
            settle(landed.at[k, :, pl.ds(0, nc - 1)], three_sem.at[k, 0])

    operands = (
        pair_state, seq_tile, index, mask, table, *gains, bias_weight_t, dist_t, *mats,
    )
    vm, dma = pltpu.VMEM, pltpu.SemaphoreType.DMA
    scratch = (
        [vm(x.shape, x.dtype) for x in operands[2:11]]
        + [vm((layers, cs, width), bf16)] * 4
        + [vm(m.shape, bf16) for m in mats[5:]]
        + [
            vm((tr, tc, ch), bf16),
            vm((tr * gap, ch), f32),
            vm((tc * tr, ch), f32),
            vm((OWN * heads, lanes), f32),
            vm((length, 128), f32),
            vm(((table.shape[0] + 127) // 128 * 128, ch), f32),
            vm((2 * bins, 2 * ch), bf16),
            vm((2, bins, 2 * ch), bf16),
            vm((half, tr, 2 * bins), f32),
            vm((hl, length, lanes), f32),
            vm((nc, tr, width), bf16),
            vm((layers, nr, 2, tr, width), bf16),
            vm((layers, heads, tc, lanes), bf16),
            vm((layers, nc, hl, tc, lanes), bf16),
            vm((tr, width), bf16),
            vm((tr, width), f32),
            vm((tr, cs), bf16),
            vm((nc, layers, width, width), bf16),
            vm((layers, owners, OWN, cs), bf16),
            vm((layers, nc, OWN, cs), bf16),
            vm((layers, OWN, cs), bf16),
            vm((layers, OWN, wide), bf16),
            vm((layers, tr, wide), bf16),
            vm((layers, tc, wide), bf16),
            vm((tr, ch), f32),
            vm((tc, 8, ch), f32),
            vm((tr, cs), bf16),
            vm((nc, OWN, width), bf16),
            vm((spans, nc, parts, depth, 2 * bins), bf16),
            vm((spans, nc, parts, depth, 2 * bins), bf16),
            vm((spans, nr, parts, parts, depth, 2 * bins), bf16),
            vm((spans, parts, nc, depth, 2 * bins), bf16),
            vm((2, parts, packed_rows, 2 * bins), f32),
            dma((9,)),
            dma((9,)),
            dma((3,)),
            dma((3,)),
            dma((layers, chunks)),
            dma((layers, chunks)),
            dma((layers, 2)),
            dma((layers, 2)),
            dma((layers, 2)),
            dma((layers, 2)),
            dma((2,)),
            dma((2,)),
            dma((spans, 2)),
            dma((spans, 2)),
            dma((spans, 2)),
        ]
    )
    return pl.pallas_call(
        kernel,
        out_shape=(
            jax.ShapeDtypeStruct((tc, bins, tr), bf16),
            jax.ShapeDtypeStruct((tr, width), bf16),
        ),
        in_specs=[any_spec()] * 20,
        out_specs=(full_spec(),) * 2,
        scratch_shapes=scratch,
        compiler_params=pltpu.CompilerParams(collective_id=0, has_side_effects=True),
    )(*operands)


def hand_over(distogram, seq_out):
    pieces = 4
    part = distogram.shape[0] // pieces

    def kernel(big_in, small_in, big_out, small_out, big, small, sem_in, sem_out):
        def moves(n):
            at = pl.ds(n * part, part)
            return (
                pltpu.make_async_copy(big_in.at[at], big.at[at], sem_in.at[n]),
                pltpu.make_async_copy(big.at[at], big_out.at[at], sem_out.at[n]),
            )

        steps = [moves(n) for n in range(pieces)] + [
            (
                pltpu.make_async_copy(small_in, small, sem_in.at[pieces]),
                pltpu.make_async_copy(small, small_out, sem_out.at[pieces]),
            )
        ]
        for take, _ in steps:
            take.start()
        for take, give in steps:
            take.wait()
            give.start()
        for _, give in steps:
            give.wait()

    arrays = (distogram, seq_out)
    shapes = [jax.ShapeDtypeStruct(x.shape, x.dtype) for x in arrays]
    return pl.pallas_call(
        kernel,
        out_shape=shapes,
        in_specs=[any_spec()] * 2,
        out_specs=[any_spec()] * 2,
        scratch_shapes=[pltpu.VMEM(x.shape, x.dtype) for x in arrays]
        + [pltpu.SemaphoreType.DMA((pieces + 1,))] * 2,
    )(*arrays)


def per_device(
    pair_state,
    seq_state,
    residue_index,
    residue_mask,
    position_table,
    attention_gain,
    bias_norm_gain,
    query_weight,
    key_weight,
    value_weight,
    gate_weight,
    out_weight,
    bias_weight,
    outer_gain,
    outer_weight,
    outer_out_weight,
    transition_gain,
    up_weight,
    down_weight,
    distance_weight,
):
    distogram, seq_out = trunk(
        pair_state,
        seq_state,
        residue_index,
        residue_mask,
        position_table,
        (attention_gain, bias_norm_gain, outer_gain, transition_gain),
        jnp.swapaxes(bias_weight, 1, 2),
        distance_weight.T,
        (
            query_weight,
            key_weight,
            value_weight,
            gate_weight,
            out_weight,
            outer_weight,
            outer_out_weight,
            up_weight,
            down_weight,
        ),
    )
    distogram, seq_out = hand_over(distogram, seq_out)
    return distogram.transpose(2, 0, 1), seq_out


def solution(mesh):
    heads_split = P(None, None, "col")
    in_specs = (
        (P("row", "col", None), P("row", "col"))
        + (P(),) * 5
        + (heads_split,) * 5
        + (P(),) * 8
    )
    out_specs = (P("row", "col", None), P("row", "col"))
    return jax.shard_map(
        per_device, mesh=mesh, in_specs=in_specs, out_specs=out_specs, check_vma=False
    )
```

```python
import jax
import jax.numpy as jnp
from jax import lax
from jax.experimental import pallas as pl
from jax.experimental.pallas import tpu as pltpu
from jax.sharding import PartitionSpec as P

HEAD_DIM = 32
RELPOS_MAX = 32
MESH = pl.DeviceIdType.MESH
OWN = 16
FAR = 1e6


def normalize(values, weight_gain):
    average = jnp.mean(values, axis=-1, keepdims=True)
    centred = values - average
    spread = jnp.mean(centred * centred, axis=-1, keepdims=True)
    return centred * lax.rsqrt(spread + 1e-05) * weight_gain


def full_spec():
    return pl.BlockSpec(memory_space=pltpu.VMEM)


def any_spec():
    return pl.BlockSpec(memory_space=pl.ANY)


def remote(source, target, send, recv, where):
    return pltpu.make_async_remote_copy(
        src_ref=source,
        dst_ref=target,
        send_sem=send,
        recv_sem=recv,
        device_id=where,
        device_id_type=MESH,
    )


def settle(ref, sem):
    pltpu.make_async_copy(ref, ref, sem).wait()


def rows_at(start, size, step):
    return pl.ds(pl.multiple_of(start, step), size)


def trunk(pair_state, pair_halves, seq_tile, index, mask, table, gains, bias_weight_t, dist_t, mats):
    nr, nc = lax.axis_size("row"), lax.axis_size("col")
    tr, tc, ch = pair_state.shape
    width = seq_tile.shape[1]
    layers, cs = mats[0].shape[:2]
    heads = bias_weight_t.shape[1]
    hl = heads // nc
    length = nr * tr
    lanes = (tr + 127) // 128 * 128
    owners, per, parts = tr // OWN, tc // OWN, tr // tc
    chunks = tc // OWN
    wide = mats[5].shape[2]
    bins = dist_t.shape[0]
    span = OWN * tc
    sub = span // nc
    score_scale = HEAD_DIM ** (-0.5)
    gap = OWN + 8
    f32, bf16 = jnp.float32, jnp.bfloat16

    def kernel(*refs):
        it = iter(refs)
        pair_hbm, halves_hbm, seq_hbm = (next(it) for _ in range(3))
        small_hbm = [next(it) for _ in range(9)]
        q_hbm, k_hbm, v_hbm, g_hbm, out_hbm = (next(it) for _ in range(5))
        late_hbm = [next(it) for _ in range(4)]
        final_ref, seq_out = (next(it) for _ in range(2))
        small_refs = [next(it) for _ in range(9)]
        index_ref, mask_ref, table_ref = small_refs[:3]
        att_gain, bias_gain, outer_gain, trans_gain, bias_w, dist_ref = small_refs[3:]
        q_w, k_w, v_w, g_w = (next(it) for _ in range(4))
        late_refs = [next(it) for _ in range(4)]
        outer_w, mix_w, up_w, down_w = late_refs
        pair_in, natural, pair_s, mixed, place, table_s = (next(it) for _ in range(6))
        head_w, mirror_s, score_s, own_b, mirror_b = (next(it) for _ in range(5))
        gathered, kv_all, bias_out, bias_all, query_s, gate_s, normed_s = (next(it) for _ in range(7))
        wrow, stage, rs_recv, new_rows, lr_s, left_all, right_all = (next(it) for _ in range(7))
        left_dup, right_rep, left_rep, right_dup, seq_next, out_stage = (next(it) for _ in range(6))
        spread_s, moved, landed = (next(it) for _ in range(3))
        load_sem, small_sem, seq_sem, w_sem, bias_send, bias_recv, kv_sem = (next(it) for _ in range(7))
        rs_sem, left_sem, right_sem, next_sem, out_sem = (next(it) for _ in range(5))
        one_sem, two_sem, three_sem = (next(it) for _ in range(3))

        row, col = lax.axis_index("row"), lax.axis_index("col")
        owner = jnp.minimum(col, owners - 1)
        holder, part_at = lax.div(col, parts), lax.rem(col, parts)

        barrier = pltpu.get_barrier_semaphore()
        for step in range(1, nc):
            pl.semaphore_signal(
                barrier, inc=1, device_id={"col": lax.rem(col + step, nc)}, device_id_type=MESH
            )
        for step in range(1, nr):
            pl.semaphore_signal(
                barrier, inc=1, device_id={"row": lax.rem(row + step, nr)}, device_id_type=MESH
            )

        @pl.when(row != holder)
        def _():
            for slot in range(per):
                pl.semaphore_signal(
                    barrier,
                    inc=1,
                    device_id={"row": holder, "col": part_at * per + slot},
                    device_id_type=MESH,
                )

        small = [
            pltpu.make_async_copy(src, dst, small_sem.at[n])
            for n, (src, dst) in enumerate(zip(small_hbm, small_refs))
        ]
        for load in small:
            load.start()
        pair_load = pltpu.make_async_copy(pair_hbm, pair_in, load_sem.at[0])
        pair_load.start()
        loads = [
            pltpu.make_async_copy(src, dst, load_sem.at[1 + n])
            for n, (src, dst) in enumerate(
                zip([k_hbm, v_hbm, q_hbm, g_hbm, *late_hbm], [k_w, v_w, q_w, g_w, *late_refs])
            )
        ]
        for load in loads:
            load.start()

        is_owner = col < owners

        @pl.when(is_owner)
        def _():
            pl.semaphore_wait(barrier, nc + 2 * nr - 3)

        @pl.when(jnp.logical_not(is_owner))
        def _():
            pl.semaphore_wait(barrier, nc + nr - 2)

        for step in range(1, nc):
            remote(
                seq_hbm,
                gathered.at[col],
                seq_sem.at[0],
                seq_sem.at[1],
                {"col": lax.rem(col + step, nc)},
            ).start()
        own_seq = pltpu.make_async_copy(seq_hbm, gathered.at[col], seq_sem.at[2])
        own_seq.start()
        for load in small:
            load.wait()
        coded = jnp.where(mask_ref[...] > 0, index_ref[...].astype(f32), FAR).reshape(1, length)
        for block in range(length // 128):
            line = coded[:, block * 128 : (block + 1) * 128]
            place[block * 128 : (block + 1) * 128, :] = jnp.broadcast_to(line, (128, 128)).T
        table_s[...] = jnp.zeros_like(table_s)
        table_s[0 : table_ref.shape[0], :] = table_ref[...].astype(f32)
        table_rows = table_s[...].astype(bf16)
        head_w[:, 0:ch] = dist_ref[...]
        head_w[:, ch : 2 * ch] = dist_ref[...]
        lane = lax.broadcasted_iota(jnp.int32, (1, ch), 1).astype(f32)
        shift = lane - (RELPOS_MAX + 1)
        least = jnp.where(lane == 0, -4 * FAR, jnp.where(lane == 1, -FAR / 2, shift))
        most = jnp.where(lane == 0, -FAR / 2, jnp.where(lane == 2 * RELPOS_MAX + 1, FAR, shift))
        low = lax.broadcasted_iota(jnp.int32, (1, ch), 1) < ch // 2

        def bias_of(layer, normed, at):
            mixed[at * heads : (at + 1) * heads, 0:tr] = lax.dot_general(
                bias_w[layer], normed, (((1,), (1,)), ((), ())), preferred_element_type=f32
            )

        def send_bias(layer, k):
            span = pl.ds(k * OWN, OWN)
            for head in range(heads):
                bias_out[layer, head, k * OWN : (k + 1) * OWN, :] = mixed[
                    pl.ds(head, OWN, stride=heads), :
                ].astype(bf16)
            for step in range(1, nc):
                peer = lax.rem(col + step, nc)
                remote(
                    bias_out.at[layer, pl.ds(peer * hl, hl), span],
                    bias_all.at[layer, col, :, span],
                    bias_send.at[layer, k],
                    bias_recv.at[layer, k],
                    {"col": peer},
                ).start()
            bias_all[layer, col, :, k * OWN : (k + 1) * OWN, :] = bias_out[
                layer, pl.ds(col * hl, hl), k * OWN : (k + 1) * OWN, :
            ]

        def enter(k):
            for i in range(tr):
                natural[i * gap : i * gap + OWN, :] = pair_in[
                    i, k * OWN : (k + 1) * OWN, :
                ].astype(f32)

            row_pos = place[rows_at(row * tr, tr, 8), :]
            hots = []
            for j in range(OWN):
                col_pos = place[pl.ds(col * tc + k * OWN + j, 1), :]
                col_pos = jnp.where(col_pos < FAR, col_pos, -FAR)
                offset = col_pos - row_pos
                hot = (offset >= least) & (offset <= most)
                hots.append(jnp.where(hot, 1.0, 0.0).astype(bf16))
            value = jnp.concatenate(
                [natural[pl.ds(j, tr, stride=gap), :] for j in range(OWN)], axis=0
            ) + jnp.dot(jnp.concatenate(hots, axis=0), table_rows, preferred_element_type=f32)
            pair_s[k * OWN * tr : (k + 1) * OWN * tr, :] = value
            normed = normalize(value, bias_gain[0:1, :]).astype(bf16)
            for j in range(OWN):
                bias_of(0, normed[j * tr : (j + 1) * tr], j)
            send_bias(0, k)

        def swap_weights(layer):
            pltpu.make_async_copy(
                out_hbm.at[layer, rows_at(col * width, width, width), :],
                wrow.at[layer, col],
                w_sem.at[layer, 2],
            ).start()
            for step in range(1, nc):
                peer = lax.rem(col + step, nc)
                remote(
                    out_hbm.at[layer, rows_at(peer * width, width, width), :],
                    wrow.at[layer, col],
                    w_sem.at[layer, 0],
                    w_sem.at[layer, 1],
                    {"col": peer},
                ).start()

        def product(layer, k, weight):
            if layer == 0:
                loads[k].wait()
            return jnp.dot(normed_s[...], weight[layer], preferred_element_type=f32)

        def project(layer, entering):
            normed_s[...] = normalize(entering, att_gain[layer : layer + 1, :]).astype(bf16)
            kv_all[layer, row, 0] = product(layer, 0, k_w).astype(bf16)
            kv_all[layer, row, 1] = product(layer, 1, v_w).astype(bf16)
            for step in range(1, nr):
                remote(
                    kv_all.at[layer, row],
                    kv_all.at[layer, row],
                    kv_sem.at[layer, 0],
                    kv_sem.at[layer, 1],
                    {"row": lax.rem(row + step, nr)},
                ).start()

        def project_rest(layer):
            query_s[...] = (product(layer, 2, q_w) * score_scale).astype(bf16)
            gate_s[...] = jax.nn.sigmoid(product(layer, 3, g_w))

        def attend(layer):
            settle(kv_all.at[layer, pl.ds(0, nr - 1)], kv_sem.at[layer, 1])
            keys = kv_all[layer, :, 0].reshape(length, width)
            values = kv_all[layer, :, 1].reshape(length, width)
            live = place[:, 0:tr] < FAR
            head_of = lax.broadcasted_iota(jnp.int32, (tr, width), 1) // HEAD_DIM
            queries = query_s[...].astype(f32)
            attended = jnp.zeros((tr, width), f32)
            for head in range(hl):
                query = jnp.where(head_of == head, queries, 0.0).astype(bf16)
                score_s[head, :, 0:tr] = lax.dot_general(
                    keys, query, (((1,), (1,)), ((), ())), preferred_element_type=f32
                )
            for k in range(chunks):
                settle(
                    bias_all.at[layer, pl.ds(0, nc - 1), :, pl.ds(k * OWN, OWN)],
                    bias_recv.at[layer, k],
                )
            for head in range(hl):
                own = head_of == head
                scores = score_s[head, :, 0:tr]
                bias = bias_all[layer, :, head].reshape(length, lanes)[:, :tr]
                scores = jnp.where(live, scores + bias.astype(f32), -jnp.inf)
                shifted = jnp.exp(scores - jnp.max(scores, axis=0, keepdims=True))
                share = (shifted * (1.0 / jnp.sum(shifted, axis=0, keepdims=True))).astype(bf16)
                mixture = lax.dot_general(
                    share, values, (((0,), (0,)), ((), ())), preferred_element_type=f32
                )
                attended = jnp.where(own, mixture, attended)
            gated = (gate_s[...] * attended).astype(bf16)
            settle(wrow.at[layer, 0], w_sem.at[layer, 2])
            settle(wrow.at[layer, pl.ds(0, nc - 1)], w_sem.at[layer, 1])
            weight = jnp.concatenate([wrow[layer, p] for p in range(nc)], axis=1)
            partial = jnp.dot(gated, weight, preferred_element_type=f32)
            stage[layer] = partial.reshape(owners, OWN, cs).astype(bf16)
            for step in range(owners):
                peer = lax.rem(col + step, owners)

                @pl.when(peer != col)
                def _(peer=peer):
                    remote(
                        stage.at[layer, peer],
                        rs_recv.at[layer, col],
                        rs_sem.at[layer, 0],
                        rs_sem.at[layer, 1],
                        {"col": peer},
                    ).start()

        def finish_rows(layer):
            at = rows_at(owner * OWN, OWN, OWN)

            @pl.when(is_owner)
            def _():
                rs_recv[layer, col] = stage[layer, owner]
                if layer == 0:
                    before = jnp.concatenate([gathered[p, at, :] for p in range(nc)], axis=1)
                else:
                    before = seq_next[at, :]
                total = before.astype(f32)
                settle(rs_recv.at[layer, pl.ds(0, nc - 1)], rs_sem.at[layer, 1])
                for p in range(nc):
                    total += rs_recv[layer, p].astype(f32)
                fresh = total.astype(bf16)
                new_rows[layer] = fresh
                outer_in = normalize(fresh.astype(f32), outer_gain[layer : layer + 1, :])
                lr_s[layer] = jnp.dot(
                    outer_in.astype(bf16), outer_w[layer], preferred_element_type=f32
                ).astype(bf16)
                slot = rows_at(lax.rem(owner, per) * OWN, OWN, OWN)
                for step in range(1, nr):
                    remote(
                        lr_s.at[layer],
                        right_all.at[layer, slot],
                        right_sem.at[layer, 0],
                        right_sem.at[layer, 1],
                        {
                            "row": lax.rem(row + step, nr),
                            "col": parts * row + lax.div(owner, per),
                        },
                    ).start()
                for step in range(1, nc):
                    remote(
                        lr_s.at[layer],
                        left_all.at[layer, at],
                        left_sem.at[layer, 0],
                        left_sem.at[layer, 1],
                        {"col": lax.rem(col + step, nc)},
                    ).start()
                left_all[layer, at, :] = lr_s[layer]
                if layer < layers - 1:
                    for step in range(1, nc):
                        remote(
                            new_rows.at[layer],
                            seq_next.at[at],
                            next_sem.at[0],
                            next_sem.at[1],
                            {"col": lax.rem(col + step, nc)},
                        ).start()
                    seq_next[at, :] = fresh
                else:
                    for p in range(nc):
                        out_stage[p] = fresh[:, p * width : (p + 1) * width]
                    for step in range(1, nc):
                        peer = lax.rem(col + step, nc)
                        remote(
                            out_stage.at[peer],
                            seq_out.at[at],
                            out_sem.at[0],
                            out_sem.at[1],
                            {"col": peer},
                        ).start()
                    seq_out[at, :] = out_stage[col]

        def from_owners(whole, most, sem):
            pl.when(is_owner)(lambda: settle(most, sem))
            pl.when(jnp.logical_not(is_owner))(lambda: settle(whole, sem))

        some = pl.ds(0, (owners - 1) * OWN)

        def sides(layer):
            from_owners(left_all.at[layer], left_all.at[layer, some], left_sem.at[layer, 1])

            @pl.when(row != holder)
            def _():
                settle(right_all.at[layer], right_sem.at[layer, 1])

            @pl.when(row == holder)
            def _():
                right_all[layer] = left_all[layer, rows_at(part_at * tc, tc, OWN), :]

            def both(values):
                turned = pltpu.roll(values, ch // 2, axis=1)
                return jnp.where(low, values, turned), jnp.where(low, turned, values)

            left, right = both(left_all[layer].astype(f32))
            left_dup[...] = left
            right_dup[layer] = right
            left, right = both(right_all[layer].astype(f32))
            left_rep[layer] = jnp.broadcast_to(left[:, None, :], (tc, 8, ch))
            right_rep[...] = jnp.broadcast_to(right[:, None, :], (tc, 8, ch))

        def features_of(left, right):
            features = jnp.where(low.reshape(1, 1, 1, ch), left * right, left - right)
            return features.reshape(-1, ch).astype(bf16)

        def passed(layer, before, features):
            middle = before + jnp.dot(features, mix_w[layer], preferred_element_type=f32)
            normed = normalize(middle, trans_gain[layer : layer + 1, :]).astype(bf16)
            hidden = jnp.maximum(
                jnp.dot(normed, up_w[layer], preferred_element_type=f32), 0.0
            ).astype(bf16)
            return (middle + jnp.dot(hidden, down_w[layer], preferred_element_type=f32)).astype(
                bf16
            )

        def update(layer, first, count):
            at = slice(first * tr, (first + count) * tr)
            right = right_rep[first : first + count][:, None]
            left = left_dup[...].reshape(1, tr // 8, 8, ch)
            fresh = passed(layer, pair_s[at, :], features_of(left, right))
            if layer == layers - 1:
                own_b[at, :] = fresh
            else:
                value = fresh.astype(f32)
                pair_s[at, :] = value
                normed = normalize(value, bias_gain[layer + 1 : layer + 2, :]).astype(bf16)
                for n in range(count):
                    bias_of(layer + 1, normed[n * tr : (n + 1) * tr], n)

        def away(g):
            pltpu.make_async_copy(
                halves_hbm.at[:, rows_at(g * span + col * sub, sub, 8), :],
                spread_s.at[g, col],
                one_sem.at[g, 2],
            ).start()
            for step in range(1, nc):
                peer = lax.rem(col + step, nc)
                remote(
                    halves_hbm.at[:, rows_at(g * span + peer * sub, sub, 8), :],
                    spread_s.at[g, col],
                    one_sem.at[g, 0],
                    one_sem.at[g, 1],
                    {"col": peer},
                ).start()

        def across(g):
            settle(spread_s.at[g, 0], one_sem.at[g, 2])
            settle(spread_s.at[g, pl.ds(0, nc - 1)], one_sem.at[g, 1])
            for step in range(nc):
                origin = lax.rem(col + step, nc)
                peer, slot = lax.div(origin, parts), lax.rem(origin, parts)
                source, target = spread_s.at[g, origin], moved.at[g, row, slot]

                @pl.when(peer != row)
                def _(source=source, target=target, peer=peer):
                    remote(
                        source, target, two_sem.at[g, 0], two_sem.at[g, 1], {"row": peer}
                    ).start()

                @pl.when(peer == row)
                def _(source=source, target=target):
                    pltpu.make_async_copy(source, target, two_sem.at[g, 1]).start()

        def home(g):
            settle(moved.at[g], two_sem.at[g, 1])
            for step in range(nr):
                origin = lax.rem(row + step, nr)
                for s in range(parts):
                    peer = origin * parts + s
                    for slot in range(parts):
                        source = moved.at[g, origin, slot, s]
                        target = landed.at[g, slot, col]

                        @pl.when(peer != col)
                        def _(source=source, target=target, peer=peer):
                            remote(
                                source,
                                target,
                                three_sem.at[g, 0],
                                three_sem.at[g, 1],
                                {"col": peer},
                            ).start()

                        @pl.when(peer == col)
                        def _(source=source, target=target):
                            pltpu.make_async_copy(source, target, three_sem.at[g, 1]).start()

        def enter_mirror(g):
            settle(landed.at[g], three_sem.at[g, 1])
            for slot in range(parts):
                col_pos = place[rows_at(row * tr + slot * tc, tc, 8), :]
                col_pos = jnp.where(col_pos < FAR, col_pos, -FAR)
                hots = []
                for j in range(OWN):
                    offset = col_pos - place[pl.ds(col * tc + g * OWN + j, 1), :]
                    hot = (offset >= least) & (offset <= most)
                    hots.append(jnp.where(hot, 1.0, 0.0))
                hots = jnp.concatenate(hots, axis=0).astype(bf16)
                mirror_s[slot, g * span : (g + 1) * span, :] = landed[g, slot].astype(
                    f32
                ).reshape(span, ch) + jnp.dot(hots, table_rows, preferred_element_type=f32)

        def update_mirror(layer, g, count):
            at = slice(g * count * tc, (g + 1) * count * tc)
            left = left_rep[layer, g * count : (g + 1) * count][:, None]
            features, before = [], []
            for slot in range(parts):
                right = right_dup[layer, slot * tc : (slot + 1) * tc, :]
                features.append(features_of(left, right.reshape(1, tc // 8, 8, ch)))
                before.append(mirror_s[slot, at, :])
            fresh = passed(
                layer, jnp.concatenate(before, axis=0), jnp.concatenate(features, axis=0)
            )
            for slot in range(parts):
                piece = fresh[slot * count * tc : (slot + 1) * count * tc]
                if layer == layers - 1:
                    mirror_b[slot, at, :] = piece
                else:
                    mirror_s[slot, at, :] = piece.astype(f32)

        def combine():
            for j in range(tc):
                mirrored = jnp.concatenate(
                    [mirror_b[slot, j * tc : (j + 1) * tc, :] for slot in range(parts)], axis=0
                )
                total = lax.dot_general(
                    head_w[...],
                    jnp.concatenate([own_b[j * tr : (j + 1) * tr, :], mirrored], axis=1),
                    (((1,), (1,)), ((), ())),
                    preferred_element_type=f32,
                )
                final_ref[j] = (total * 0.5).astype(bf16)

        swap_weights(0)
        pair_load.wait()
        enter(0)
        own_seq.wait()
        settle(gathered.at[pl.ds(0, nc - 1)], seq_sem.at[1])
        project(0, jnp.concatenate([gathered[p] for p in range(nc)], axis=1).astype(f32))
        for k in range(1, chunks):
            enter(k)
        away(0)
        project_rest(0)
        for layer in range(layers):
            last = layer == layers - 1
            attend(layer)
            if layer == 0:
                for load in loads[4:]:
                    load.wait()
                away(1)
            if last:
                across(2)
                enter_mirror(0)
                for below in range(layers - 1):
                    update_mirror(below, 0, OWN)
            finish_rows(layer)
            if layer == 0:
                across(0)
                swap_weights(1)
            if last:
                home(1)
            sides(layer)
            if not last:
                away(2)
                for k in range(chunks):
                    update(layer, k * OWN, OWN)
                    send_bias(layer + 1, k)
                    if k == 0:
                        from_owners(seq_next, seq_next.at[some], next_sem.at[1])
                        project(layer + 1, seq_next[...].astype(f32))
                        across(1)
                home(0)
                project_rest(layer + 1)
        update(layers - 1, 0, OWN)
        home(2)
        update(layers - 1, OWN, tc - OWN)
        update_mirror(layers - 1, 0, OWN)
        enter_mirror(1)
        for below in range(layers - 1):
            update_mirror(below, 1, OWN)
        update_mirror(layers - 1, 1, OWN)
        enter_mirror(2)
        for below in range(layers - 1):
            update_mirror(below, 2, OWN)
        update_mirror(layers - 1, 2, OWN)
        combine()
        from_owners(seq_out, seq_out.at[some], out_sem.at[1])

        settle(gathered.at[pl.ds(0, nc - 1)], seq_sem.at[0])
        for layer in range(layers):
            settle(wrow.at[layer, pl.ds(0, nc - 1)], w_sem.at[layer, 0])
            for k in range(chunks):
                settle(
                    bias_out.at[layer, pl.ds(0, (nc - 1) * hl), pl.ds(k * OWN, OWN)],
                    bias_send.at[layer, k],
                )
            settle(kv_all.at[layer, pl.ds(0, nr - 1)], kv_sem.at[layer, 0])

            from_owners(
                stage.at[layer], stage.at[layer, pl.ds(0, owners - 1)], rs_sem.at[layer, 0]
            )

            @pl.when(is_owner)
            def _(layer=layer):
                settle(
                    rs_recv.at[layer, pl.ds(0, nr - 1), :, pl.ds(0, wide)],
                    right_sem.at[layer, 0],
                )
                settle(
                    rs_recv.at[layer, pl.ds(0, nc - 1), :, pl.ds(0, wide)],
                    left_sem.at[layer, 0],
                )
                if layer < layers - 1:
                    settle(rs_recv.at[layer, pl.ds(0, nc - 1)], next_sem.at[0])
                else:
                    settle(out_stage.at[pl.ds(0, nc - 1)], out_sem.at[0])

        for g in range(chunks):
            settle(spread_s.at[g, pl.ds(0, nc - 1)], one_sem.at[g, 0])
            settle(spread_s.at[g, pl.ds(0, nc - parts)], two_sem.at[g, 0])
            settle(landed.at[g, :, pl.ds(0, nc - 1)], three_sem.at[g, 0])

    operands = (
        pair_state, pair_halves, seq_tile, index, mask, table, *gains, bias_weight_t, dist_t, *mats,
    )
    vm, dma = pltpu.VMEM, pltpu.SemaphoreType.DMA
    scratch = (
        [vm(x.shape, x.dtype) for x in operands[3:12]]
        + [vm((layers, cs, width), bf16)] * 4
        + [vm(m.shape, bf16) for m in mats[5:]]
        + [
            vm((tr, tc, ch), bf16),
            vm((tr * gap, ch), f32),
            vm((tc * tr, ch), f32),
            vm((OWN * heads, lanes), f32),
            vm((length, 128), f32),
            vm(((table.shape[0] + 127) // 128 * 128, ch), f32),
            vm((bins, 2 * ch), bf16),
            vm((parts, tc * tc, ch), f32),
            vm((hl, length, lanes), f32),
            vm((tc * tr, ch), bf16),
            vm((parts, tc * tc, ch), bf16),
            vm((nc, tr, width), bf16),
            vm((layers, nr, 2, tr, width), bf16),
            vm((layers, heads, tc, lanes), bf16),
            vm((layers, nc, hl, tc, lanes), bf16),
            vm((tr, width), bf16),
            vm((tr, width), f32),
            vm((tr, cs), bf16),
            vm((layers, nc, width, width), bf16),
            vm((layers, owners, OWN, cs), bf16),
            vm((layers, nc, OWN, cs), bf16),
            vm((layers, OWN, cs), bf16),
            vm((layers, OWN, wide), bf16),
            vm((layers, tr, wide), bf16),
            vm((layers, tc, wide), bf16),
            vm((tr, ch), f32),
            vm((tc, 8, ch), f32),
            vm((layers, tc, 8, ch), f32),
            vm((layers, tr, ch), f32),
            vm((tr, cs), bf16),
            vm((nc, OWN, width), bf16),
            vm((chunks, nc, parts, sub, ch), bf16),
            vm((chunks, nr, parts, parts, sub, ch), bf16),
            vm((chunks, parts, nc, sub, ch), bf16),
            dma((9,)),
            dma((9,)),
            dma((3,)),
            dma((layers, 3)),
            dma((layers, chunks)),
            dma((layers, chunks)),
            dma((layers, 2)),
            dma((layers, 2)),
            dma((layers, 2)),
            dma((layers, 2)),
            dma((2,)),
            dma((2,)),
            dma((chunks, 3)),
            dma((chunks, 2)),
            dma((chunks, 2)),
        ]
    )
    return pl.pallas_call(
        kernel,
        out_shape=(
            jax.ShapeDtypeStruct((tc, bins, tr), bf16),
            jax.ShapeDtypeStruct((tr, width), bf16),
        ),
        in_specs=[any_spec()] * len(operands),
        out_specs=(full_spec(),) * 2,
        scratch_shapes=scratch,
        compiler_params=pltpu.CompilerParams(collective_id=0, has_side_effects=True),
    )(*operands)


def hand_over(distogram, seq_out):
    pieces = 4
    part = distogram.shape[0] // pieces

    def kernel(big_in, small_in, big_out, small_out, big, small, sem_in, sem_out):
        def moves(n):
            at = pl.ds(n * part, part)
            return (
                pltpu.make_async_copy(big_in.at[at], big.at[at], sem_in.at[n]),
                pltpu.make_async_copy(big.at[at], big_out.at[at], sem_out.at[n]),
            )

        steps = [moves(n) for n in range(pieces)] + [
            (
                pltpu.make_async_copy(small_in, small, sem_in.at[pieces]),
                pltpu.make_async_copy(small, small_out, sem_out.at[pieces]),
            )
        ]
        for take, _ in steps:
            take.start()
        for take, give in steps:
            take.wait()
            give.start()
        for _, give in steps:
            give.wait()

    arrays = (distogram, seq_out)
    shapes = [jax.ShapeDtypeStruct(x.shape, x.dtype) for x in arrays]
    return pl.pallas_call(
        kernel,
        out_shape=shapes,
        in_specs=[any_spec()] * 2,
        out_specs=[any_spec()] * 2,
        scratch_shapes=[pltpu.VMEM(x.shape, x.dtype) for x in arrays]
        + [pltpu.SemaphoreType.DMA((pieces + 1,))] * 2,
    )(*arrays)


def per_device(
    pair_state,
    seq_state,
    residue_index,
    residue_mask,
    position_table,
    attention_gain,
    bias_norm_gain,
    query_weight,
    key_weight,
    value_weight,
    gate_weight,
    out_weight,
    bias_weight,
    outer_gain,
    outer_weight,
    outer_out_weight,
    transition_gain,
    up_weight,
    down_weight,
    distance_weight,
):
    parts = pair_state.shape[0] // pair_state.shape[1]
    distogram, seq_out = trunk(
        pair_state,
        pair_state.reshape(parts, -1, pair_state.shape[2]),
        seq_state,
        residue_index,
        residue_mask,
        position_table,
        (attention_gain, bias_norm_gain, outer_gain, transition_gain),
        jnp.swapaxes(bias_weight, 1, 2),
        distance_weight.T,
        (
            query_weight,
            key_weight,
            value_weight,
            gate_weight,
            out_weight,
            outer_weight,
            outer_out_weight,
            up_weight,
            down_weight,
        ),
    )
    distogram, seq_out = hand_over(distogram, seq_out)
    return distogram.transpose(2, 0, 1), seq_out


def solution(mesh):
    heads_split = P(None, None, "col")
    in_specs = (
        (P("row", "col", None), P("row", "col"))
        + (P(),) * 5
        + (heads_split,) * 5
        + (P(),) * 8
    )
    out_specs = (P("row", "col", None), P("row", "col"))
    return jax.shard_map(
        per_device, mesh=mesh, in_specs=in_specs, out_specs=out_specs, check_vma=False
    )
```

```python
import jax
import jax.numpy as jnp
from jax import lax
from jax.experimental import pallas as pl
from jax.experimental.pallas import tpu as pltpu
from jax.sharding import PartitionSpec as P

HEAD_DIM = 32
RELPOS_MAX = 32
MESH = pl.DeviceIdType.MESH
OWN = 16
FAR = 1e6


def normalize(values, weight_gain):
    average = jnp.mean(values, axis=-1, keepdims=True)
    centred = values - average
    spread = jnp.mean(centred * centred, axis=-1, keepdims=True)
    return centred * lax.rsqrt(spread + 1e-05) * weight_gain


def full_spec():
    return pl.BlockSpec(memory_space=pltpu.VMEM)


def any_spec():
    return pl.BlockSpec(memory_space=pl.ANY)


def remote(source, target, send, recv, where):
    return pltpu.make_async_remote_copy(
        src_ref=source,
        dst_ref=target,
        send_sem=send,
        recv_sem=recv,
        device_id=where,
        device_id_type=MESH,
    )


def settle(ref, sem):
    pltpu.make_async_copy(ref, ref, sem).wait()


def rows_at(start, size, step):
    return pl.ds(pl.multiple_of(start, step), size)


def trunk(pair_state, pair_halves, seq_tile, index, mask, table, gains, bias_weight_t, dist_t, mats):
    nr, nc = lax.axis_size("row"), lax.axis_size("col")
    tr, tc, ch = pair_state.shape
    width = seq_tile.shape[1]
    layers, cs = mats[0].shape[:2]
    heads = bias_weight_t.shape[1]
    hl = heads // nc
    length = nr * tr
    lanes = (tr + 127) // 128 * 128
    owners, per, parts = tr // OWN, tc // OWN, tr // tc
    chunks = tc // OWN
    wide = mats[5].shape[2]
    bins = dist_t.shape[0]
    span = OWN * tc
    sub = span // nc
    score_scale = HEAD_DIM ** (-0.5)
    gap = OWN + 8
    f32, bf16 = jnp.float32, jnp.bfloat16

    def kernel(*refs):
        it = iter(refs)
        pair_hbm, halves_hbm, seq_hbm = (next(it) for _ in range(3))
        small_hbm = [next(it) for _ in range(9)]
        q_hbm, k_hbm, v_hbm, g_hbm, out_hbm = (next(it) for _ in range(5))
        late_hbm = [next(it) for _ in range(4)]
        final_ref, seq_out = (next(it) for _ in range(2))
        small_refs = [next(it) for _ in range(9)]
        index_ref, mask_ref, table_ref = small_refs[:3]
        att_gain, bias_gain, outer_gain, trans_gain, bias_w, dist_ref = small_refs[3:]
        q_w, k_w, v_w, g_w = (next(it) for _ in range(4))
        late_refs = [next(it) for _ in range(4)]
        outer_w, mix_w, up_w, down_w = late_refs
        pair_in, natural, pair_s, mixed, place, table_s = (next(it) for _ in range(6))
        head_w, mirror_s, score_s, own_b, mirror_b = (next(it) for _ in range(5))
        gathered, kv_all, bias_out, bias_all, query_s, gate_s, normed_s = (next(it) for _ in range(7))
        wrow, stage, rs_recv, new_rows, lr_s, left_all, right_all = (next(it) for _ in range(7))
        left_dup, right_rep, left_rep, right_dup, seq_next, out_stage = (next(it) for _ in range(6))
        spread_s, moved, landed = (next(it) for _ in range(3))
        load_sem, small_sem, seq_sem, w_sem, bias_send, bias_recv, kv_sem = (next(it) for _ in range(7))
        rs_sem, left_sem, right_sem, next_sem, out_sem = (next(it) for _ in range(5))
        one_sem, two_sem, three_sem = (next(it) for _ in range(3))

        row, col = lax.axis_index("row"), lax.axis_index("col")
        owner = jnp.minimum(col, owners - 1)
        holder, part_at = lax.div(col, parts), lax.rem(col, parts)

        barrier = pltpu.get_barrier_semaphore()
        for step in range(1, nc):
            pl.semaphore_signal(
                barrier, inc=1, device_id={"col": lax.rem(col + step, nc)}, device_id_type=MESH
            )
        for step in range(1, nr):
            pl.semaphore_signal(
                barrier, inc=1, device_id={"row": lax.rem(row + step, nr)}, device_id_type=MESH
            )

        @pl.when(row != holder)
        def _():
            for slot in range(per):
                pl.semaphore_signal(
                    barrier,
                    inc=1,
                    device_id={"row": holder, "col": part_at * per + slot},
                    device_id_type=MESH,
                )

        small = [
            pltpu.make_async_copy(src, dst, small_sem.at[n])
            for n, (src, dst) in enumerate(zip(small_hbm, small_refs))
        ]
        for load in small:
            load.start()
        pair_load = pltpu.make_async_copy(pair_hbm, pair_in, load_sem.at[0])
        pair_load.start()
        loads = [
            pltpu.make_async_copy(src, dst, load_sem.at[1 + n])
            for n, (src, dst) in enumerate(
                zip([k_hbm, v_hbm, q_hbm, g_hbm, *late_hbm], [k_w, v_w, q_w, g_w, *late_refs])
            )
        ]
        for load in loads:
            load.start()

        is_owner = col < owners

        @pl.when(is_owner)
        def _():
            pl.semaphore_wait(barrier, nc + 2 * nr - 3)

        @pl.when(jnp.logical_not(is_owner))
        def _():
            pl.semaphore_wait(barrier, nc + nr - 2)

        for step in range(1, nc):
            remote(
                seq_hbm,
                gathered.at[col],
                seq_sem.at[0],
                seq_sem.at[1],
                {"col": lax.rem(col + step, nc)},
            ).start()
        own_seq = pltpu.make_async_copy(seq_hbm, gathered.at[col], seq_sem.at[2])
        own_seq.start()
        for load in small:
            load.wait()
        coded = jnp.where(mask_ref[...] > 0, index_ref[...].astype(f32), FAR).reshape(1, length)
        for block in range(length // 128):
            line = coded[:, block * 128 : (block + 1) * 128]
            place[block * 128 : (block + 1) * 128, :] = jnp.broadcast_to(line, (128, 128)).T
        table_s[...] = jnp.zeros_like(table_s)
        table_s[0 : table_ref.shape[0], :] = table_ref[...].astype(f32)
        table_rows = table_s[...].astype(bf16)
        head_w[:, 0:ch] = dist_ref[...]
        head_w[:, ch : 2 * ch] = dist_ref[...]
        lane = lax.broadcasted_iota(jnp.int32, (1, ch), 1).astype(f32)
        shift = lane - (RELPOS_MAX + 1)
        least = jnp.where(lane == 0, -4 * FAR, jnp.where(lane == 1, -FAR / 2, shift))
        most = jnp.where(lane == 0, -FAR / 2, jnp.where(lane == 2 * RELPOS_MAX + 1, FAR, shift))
        low = lax.broadcasted_iota(jnp.int32, (1, ch), 1) < ch // 2

        def bias_of(layer, normed, at):
            mixed[at * heads : (at + 1) * heads, 0:tr] = lax.dot_general(
                bias_w[layer], normed, (((1,), (1,)), ((), ())), preferred_element_type=f32
            )

        def send_bias(layer, k):
            span = pl.ds(k * OWN, OWN)
            for head in range(heads):
                bias_out[layer, head, k * OWN : (k + 1) * OWN, :] = mixed[
                    pl.ds(head, OWN, stride=heads), :
                ].astype(bf16)
            for step in range(1, nc):
                peer = lax.rem(col + step, nc)
                remote(
                    bias_out.at[layer, pl.ds(peer * hl, hl), span],
                    bias_all.at[layer, col, :, span],
                    bias_send.at[layer, k],
                    bias_recv.at[layer, k],
                    {"col": peer},
                ).start()
            bias_all[layer, col, :, k * OWN : (k + 1) * OWN, :] = bias_out[
                layer, pl.ds(col * hl, hl), k * OWN : (k + 1) * OWN, :
            ]

        def enter(k):
            for i in range(tr):
                natural[i * gap : i * gap + OWN, :] = pair_in[
                    i, k * OWN : (k + 1) * OWN, :
                ].astype(f32)

            row_pos = place[rows_at(row * tr, tr, 8), :]
            hots = []
            for j in range(OWN):
                col_pos = place[pl.ds(col * tc + k * OWN + j, 1), :]
                col_pos = jnp.where(col_pos < FAR, col_pos, -FAR)
                offset = col_pos - row_pos
                hot = (offset >= least) & (offset <= most)
                hots.append(jnp.where(hot, 1.0, 0.0).astype(bf16))
            value = jnp.concatenate(
                [natural[pl.ds(j, tr, stride=gap), :] for j in range(OWN)], axis=0
            ) + jnp.dot(jnp.concatenate(hots, axis=0), table_rows, preferred_element_type=f32)
            pair_s[k * OWN * tr : (k + 1) * OWN * tr, :] = value
            normed = normalize(value, bias_gain[0:1, :]).astype(bf16)
            for j in range(OWN):
                bias_of(0, normed[j * tr : (j + 1) * tr], j)
            send_bias(0, k)

        def swap_weights(layer):
            pltpu.make_async_copy(
                out_hbm.at[layer, rows_at(col * width, width, width), :],
                wrow.at[layer, col],
                w_sem.at[layer, 2],
            ).start()
            for step in range(1, nc):
                peer = lax.rem(col + step, nc)
                remote(
                    out_hbm.at[layer, rows_at(peer * width, width, width), :],
                    wrow.at[layer, col],
                    w_sem.at[layer, 0],
                    w_sem.at[layer, 1],
                    {"col": peer},
                ).start()

        def product(layer, k, weight):
            if layer == 0:
                loads[k].wait()
            return jnp.dot(normed_s[...], weight[layer], preferred_element_type=f32)

        def project(layer, entering):
            normed_s[...] = normalize(entering, att_gain[layer : layer + 1, :]).astype(bf16)
            kv_all[layer, row, 0] = product(layer, 0, k_w).astype(bf16)
            kv_all[layer, row, 1] = product(layer, 1, v_w).astype(bf16)
            for step in range(1, nr):
                remote(
                    kv_all.at[layer, row],
                    kv_all.at[layer, row],
                    kv_sem.at[layer, 0],
                    kv_sem.at[layer, 1],
                    {"row": lax.rem(row + step, nr)},
                ).start()

        def project_rest(layer):
            query_s[...] = (product(layer, 2, q_w) * score_scale).astype(bf16)
            gate_s[...] = jax.nn.sigmoid(product(layer, 3, g_w))

        def attend(layer):
            settle(kv_all.at[layer, pl.ds(0, nr - 1)], kv_sem.at[layer, 1])
            keys = kv_all[layer, :, 0].reshape(length, width)
            values = kv_all[layer, :, 1].reshape(length, width)
            live = place[:, 0:tr] < FAR
            head_of = lax.broadcasted_iota(jnp.int32, (tr, width), 1) // HEAD_DIM
            queries = query_s[...].astype(f32)
            attended = jnp.zeros((tr, width), f32)
            for head in range(hl):
                query = jnp.where(head_of == head, queries, 0.0).astype(bf16)
                score_s[head, :, 0:tr] = lax.dot_general(
                    keys, query, (((1,), (1,)), ((), ())), preferred_element_type=f32
                )
            for k in range(chunks):
                settle(
                    bias_all.at[layer, pl.ds(0, nc - 1), :, pl.ds(k * OWN, OWN)],
                    bias_recv.at[layer, k],
                )
            for head in range(hl):
                own = head_of == head
                scores = score_s[head, :, 0:tr]
                bias = bias_all[layer, :, head].reshape(length, lanes)[:, :tr]
                scores = jnp.where(live, scores + bias.astype(f32), -jnp.inf)
                shifted = jnp.exp(scores - jnp.max(scores, axis=0, keepdims=True))
                share = (shifted * (1.0 / jnp.sum(shifted, axis=0, keepdims=True))).astype(bf16)
                mixture = lax.dot_general(
                    share, values, (((0,), (0,)), ((), ())), preferred_element_type=f32
                )
                attended = jnp.where(own, mixture, attended)
            gated = (gate_s[...] * attended).astype(bf16)
            settle(wrow.at[layer, 0], w_sem.at[layer, 2])
            settle(wrow.at[layer, pl.ds(0, nc - 1)], w_sem.at[layer, 1])
            weight = jnp.concatenate([wrow[layer, p] for p in range(nc)], axis=1)
            partial = jnp.dot(gated, weight, preferred_element_type=f32)
            stage[layer] = partial.reshape(owners, OWN, cs).astype(bf16)
            for step in range(owners):
                peer = lax.rem(col + step, owners)

                @pl.when(peer != col)
                def _(peer=peer):
                    remote(
                        stage.at[layer, peer],
                        rs_recv.at[layer, col],
                        rs_sem.at[layer, 0],
                        rs_sem.at[layer, 1],
                        {"col": peer},
                    ).start()

        def finish_rows(layer):
            at = rows_at(owner * OWN, OWN, OWN)

            @pl.when(is_owner)
            def _():
                rs_recv[layer, col] = stage[layer, owner]
                if layer == 0:
                    before = jnp.concatenate([gathered[p, at, :] for p in range(nc)], axis=1)
                else:
                    before = seq_next[at, :]
                total = before.astype(f32)
                settle(rs_recv.at[layer, pl.ds(0, nc - 1)], rs_sem.at[layer, 1])
                for p in range(nc):
                    total += rs_recv[layer, p].astype(f32)
                fresh = total.astype(bf16)
                new_rows[layer] = fresh
                outer_in = normalize(fresh.astype(f32), outer_gain[layer : layer + 1, :])
                lr_s[layer] = jnp.dot(
                    outer_in.astype(bf16), outer_w[layer], preferred_element_type=f32
                ).astype(bf16)
                slot = rows_at(lax.rem(owner, per) * OWN, OWN, OWN)
                for step in range(1, nr):
                    remote(
                        lr_s.at[layer],
                        right_all.at[layer, slot],
                        right_sem.at[layer, 0],
                        right_sem.at[layer, 1],
                        {
                            "row": lax.rem(row + step, nr),
                            "col": parts * row + lax.div(owner, per),
                        },
                    ).start()
                for step in range(1, nc):
                    remote(
                        lr_s.at[layer],
                        left_all.at[layer, at],
                        left_sem.at[layer, 0],
                        left_sem.at[layer, 1],
                        {"col": lax.rem(col + step, nc)},
                    ).start()
                left_all[layer, at, :] = lr_s[layer]
                if layer < layers - 1:
                    for step in range(1, nc):
                        remote(
                            new_rows.at[layer],
                            seq_next.at[at],
                            next_sem.at[0],
                            next_sem.at[1],
                            {"col": lax.rem(col + step, nc)},
                        ).start()
                    seq_next[at, :] = fresh
                else:
                    for p in range(nc):
                        out_stage[p] = fresh[:, p * width : (p + 1) * width]
                    for step in range(1, nc):
                        peer = lax.rem(col + step, nc)
                        remote(
                            out_stage.at[peer],
                            seq_out.at[at],
                            out_sem.at[0],
                            out_sem.at[1],
                            {"col": peer},
                        ).start()
                    seq_out[at, :] = out_stage[col]

        def from_owners(whole, most, sem):
            pl.when(is_owner)(lambda: settle(most, sem))
            pl.when(jnp.logical_not(is_owner))(lambda: settle(whole, sem))

        some = pl.ds(0, (owners - 1) * OWN)

        def sides(layer):
            from_owners(left_all.at[layer], left_all.at[layer, some], left_sem.at[layer, 1])

            @pl.when(row != holder)
            def _():
                settle(right_all.at[layer], right_sem.at[layer, 1])

            @pl.when(row == holder)
            def _():
                right_all[layer] = left_all[layer, rows_at(part_at * tc, tc, OWN), :]

            def both(values):
                turned = pltpu.roll(values, ch // 2, axis=1)
                return jnp.where(low, values, turned), jnp.where(low, turned, values)

            left, right = both(left_all[layer].astype(f32))
            left_dup[...] = left
            right_dup[layer] = right
            left, right = both(right_all[layer].astype(f32))
            left_rep[layer] = jnp.broadcast_to(left[:, None, :], (tc, 8, ch))
            right_rep[...] = jnp.broadcast_to(right[:, None, :], (tc, 8, ch))

        def features_of(left, right):
            features = jnp.where(low.reshape(1, 1, 1, ch), left * right, left - right)
            return features.reshape(-1, ch).astype(bf16)

        def passed(layer, before, features):
            middle = before + jnp.dot(features, mix_w[layer], preferred_element_type=f32)
            normed = normalize(middle, trans_gain[layer : layer + 1, :]).astype(bf16)
            hidden = jnp.maximum(
                jnp.dot(normed, up_w[layer], preferred_element_type=f32), 0.0
            ).astype(bf16)
            return (middle + jnp.dot(hidden, down_w[layer], preferred_element_type=f32)).astype(
                bf16
            )

        def update(layer, first, count):
            at = slice(first * tr, (first + count) * tr)
            right = right_rep[first : first + count][:, None]
            left = left_dup[...].reshape(1, tr // 8, 8, ch)
            fresh = passed(layer, pair_s[at, :], features_of(left, right))
            if layer == layers - 1:
                own_b[at, :] = fresh
            else:
                value = fresh.astype(f32)
                pair_s[at, :] = value
                normed = normalize(value, bias_gain[layer + 1 : layer + 2, :]).astype(bf16)
                for n in range(count):
                    bias_of(layer + 1, normed[n * tr : (n + 1) * tr], n)

        def away(g):
            pltpu.make_async_copy(
                halves_hbm.at[:, rows_at(g * span + col * sub, sub, 8), :],
                spread_s.at[g, col],
                one_sem.at[g, 2],
            ).start()
            for step in range(1, nc):
                peer = lax.rem(col + step, nc)
                remote(
                    halves_hbm.at[:, rows_at(g * span + peer * sub, sub, 8), :],
                    spread_s.at[g, col],
                    one_sem.at[g, 0],
                    one_sem.at[g, 1],
                    {"col": peer},
                ).start()

        def across(g):
            settle(spread_s.at[g, 0], one_sem.at[g, 2])
            settle(spread_s.at[g, pl.ds(0, nc - 1)], one_sem.at[g, 1])
            for step in range(nc):
                origin = lax.rem(col + step, nc)
                peer, slot = lax.div(origin, parts), lax.rem(origin, parts)
                source, target = spread_s.at[g, origin], moved.at[g, row, slot]

                @pl.when(peer != row)
                def _(source=source, target=target, peer=peer):
                    remote(
                        source, target, two_sem.at[g, 0], two_sem.at[g, 1], {"row": peer}
                    ).start()

                @pl.when(peer == row)
                def _(source=source, target=target):
                    pltpu.make_async_copy(source, target, two_sem.at[g, 1]).start()

        def home(g):
            settle(moved.at[g], two_sem.at[g, 1])
            for step in range(nr):
                origin = lax.rem(row + step, nr)
                for s in range(parts):
                    peer = origin * parts + s
                    for slot in range(parts):
                        source = moved.at[g, origin, slot, s]
                        target = landed.at[g, slot, col]

                        @pl.when(peer != col)
                        def _(source=source, target=target, peer=peer):
                            remote(
                                source,
                                target,
                                three_sem.at[g, 0],
                                three_sem.at[g, 1],
                                {"col": peer},
                            ).start()

                        @pl.when(peer == col)
                        def _(source=source, target=target):
                            pltpu.make_async_copy(source, target, three_sem.at[g, 1]).start()

        def enter_mirror(g):
            settle(landed.at[g], three_sem.at[g, 1])
            for slot in range(parts):
                col_pos = place[rows_at(row * tr + slot * tc, tc, 8), :]
                col_pos = jnp.where(col_pos < FAR, col_pos, -FAR)
                hots = []
                for j in range(OWN):
                    offset = col_pos - place[pl.ds(col * tc + g * OWN + j, 1), :]
                    hot = (offset >= least) & (offset <= most)
                    hots.append(jnp.where(hot, 1.0, 0.0))
                hots = jnp.concatenate(hots, axis=0).astype(bf16)
                mirror_s[slot, g * span : (g + 1) * span, :] = landed[g, slot].astype(
                    f32
                ).reshape(span, ch) + jnp.dot(hots, table_rows, preferred_element_type=f32)

        def update_mirror(layer, g, count):
            at = slice(g * count * tc, (g + 1) * count * tc)
            left = left_rep[layer, g * count : (g + 1) * count][:, None]
            features, before = [], []
            for slot in range(parts):
                right = right_dup[layer, slot * tc : (slot + 1) * tc, :]
                features.append(features_of(left, right.reshape(1, tc // 8, 8, ch)))
                before.append(mirror_s[slot, at, :])
            fresh = passed(
                layer, jnp.concatenate(before, axis=0), jnp.concatenate(features, axis=0)
            )
            for slot in range(parts):
                piece = fresh[slot * count * tc : (slot + 1) * count * tc]
                if layer == layers - 1:
                    mirror_b[slot, at, :] = piece
                else:
                    mirror_s[slot, at, :] = piece.astype(f32)

        def combine():
            for j in range(tc):
                mirrored = jnp.concatenate(
                    [mirror_b[slot, j * tc : (j + 1) * tc, :] for slot in range(parts)], axis=0
                )
                total = lax.dot_general(
                    head_w[...],
                    jnp.concatenate([own_b[j * tr : (j + 1) * tr, :], mirrored], axis=1),
                    (((1,), (1,)), ((), ())),
                    preferred_element_type=f32,
                )
                final_ref[j] = (total * 0.5).astype(bf16)

        swap_weights(0)
        pair_load.wait()
        enter(0)
        own_seq.wait()
        settle(gathered.at[pl.ds(0, nc - 1)], seq_sem.at[1])
        project(0, jnp.concatenate([gathered[p] for p in range(nc)], axis=1).astype(f32))
        for k in range(1, chunks):
            enter(k)
        away(0)
        project_rest(0)
        for layer in range(layers):
            last = layer == layers - 1
            attend(layer)
            if layer == 0:
                for load in loads[4:]:
                    load.wait()
                away(1)
            if last:
                across(2)
                enter_mirror(0)
                for below in range(layers - 1):
                    update_mirror(below, 0, OWN)
            finish_rows(layer)
            if layer == 0:
                across(0)
            if last:
                home(1)
            sides(layer)
            if not last:
                swap_weights(1)
                away(2)
                for k in range(chunks):
                    update(layer, k * OWN, OWN)
                    send_bias(layer + 1, k)
                    if k == 0:
                        from_owners(seq_next, seq_next.at[some], next_sem.at[1])
                        project(layer + 1, seq_next[...].astype(f32))
                        across(1)
                home(0)
                project_rest(layer + 1)
        update(layers - 1, 0, OWN)
        home(2)
        update(layers - 1, OWN, tc - OWN)
        enter_mirror(1)
        for below in range(layers - 1):
            update_mirror(below, 1, OWN)
        update_mirror(layers - 1, 0, 2 * OWN)
        enter_mirror(2)
        for below in range(layers - 1):
            update_mirror(below, 2, OWN)
        update_mirror(layers - 1, 2, OWN)
        combine()
        from_owners(seq_out, seq_out.at[some], out_sem.at[1])

        settle(gathered.at[pl.ds(0, nc - 1)], seq_sem.at[0])
        for layer in range(layers):
            settle(wrow.at[layer, pl.ds(0, nc - 1)], w_sem.at[layer, 0])
            for k in range(chunks):
                settle(
                    bias_out.at[layer, pl.ds(0, (nc - 1) * hl), pl.ds(k * OWN, OWN)],
                    bias_send.at[layer, k],
                )
            settle(kv_all.at[layer, pl.ds(0, nr - 1)], kv_sem.at[layer, 0])

            from_owners(
                stage.at[layer], stage.at[layer, pl.ds(0, owners - 1)], rs_sem.at[layer, 0]
            )

            @pl.when(is_owner)
            def _(layer=layer):
                settle(
                    rs_recv.at[layer, pl.ds(0, nr - 1), :, pl.ds(0, wide)],
                    right_sem.at[layer, 0],
                )
                settle(
                    rs_recv.at[layer, pl.ds(0, nc - 1), :, pl.ds(0, wide)],
                    left_sem.at[layer, 0],
                )
                if layer < layers - 1:
                    settle(rs_recv.at[layer, pl.ds(0, nc - 1)], next_sem.at[0])
                else:
                    settle(out_stage.at[pl.ds(0, nc - 1)], out_sem.at[0])

        for g in range(chunks):
            settle(spread_s.at[g, pl.ds(0, nc - 1)], one_sem.at[g, 0])
            settle(spread_s.at[g, pl.ds(0, nc - parts)], two_sem.at[g, 0])
            settle(landed.at[g, :, pl.ds(0, nc - 1)], three_sem.at[g, 0])

    operands = (
        pair_state, pair_halves, seq_tile, index, mask, table, *gains, bias_weight_t, dist_t, *mats,
    )
    vm, dma = pltpu.VMEM, pltpu.SemaphoreType.DMA
    scratch = (
        [vm(x.shape, x.dtype) for x in operands[3:12]]
        + [vm((layers, cs, width), bf16)] * 4
        + [vm(m.shape, bf16) for m in mats[5:]]
        + [
            vm((tr, tc, ch), bf16),
            vm((tr * gap, ch), f32),
            vm((tc * tr, ch), f32),
            vm((OWN * heads, lanes), f32),
            vm((length, 128), f32),
            vm(((table.shape[0] + 127) // 128 * 128, ch), f32),
            vm((bins, 2 * ch), bf16),
            vm((parts, tc * tc, ch), f32),
            vm((hl, length, lanes), f32),
            vm((tc * tr, ch), bf16),
            vm((parts, tc * tc, ch), bf16),
            vm((nc, tr, width), bf16),
            vm((layers, nr, 2, tr, width), bf16),
            vm((layers, heads, tc, lanes), bf16),
            vm((layers, nc, hl, tc, lanes), bf16),
            vm((tr, width), bf16),
            vm((tr, width), f32),
            vm((tr, cs), bf16),
            vm((layers, nc, width, width), bf16),
            vm((layers, owners, OWN, cs), bf16),
            vm((layers, nc, OWN, cs), bf16),
            vm((layers, OWN, cs), bf16),
            vm((layers, OWN, wide), bf16),
            vm((layers, tr, wide), bf16),
            vm((layers, tc, wide), bf16),
            vm((tr, ch), f32),
            vm((tc, 8, ch), f32),
            vm((layers, tc, 8, ch), f32),
            vm((layers, tr, ch), f32),
            vm((tr, cs), bf16),
            vm((nc, OWN, width), bf16),
            vm((chunks, nc, parts, sub, ch), bf16),
            vm((chunks, nr, parts, parts, sub, ch), bf16),
            vm((chunks, parts, nc, sub, ch), bf16),
            dma((9,)),
            dma((9,)),
            dma((3,)),
            dma((layers, 3)),
            dma((layers, chunks)),
            dma((layers, chunks)),
            dma((layers, 2)),
            dma((layers, 2)),
            dma((layers, 2)),
            dma((layers, 2)),
            dma((2,)),
            dma((2,)),
            dma((chunks, 3)),
            dma((chunks, 2)),
            dma((chunks, 2)),
        ]
    )
    return pl.pallas_call(
        kernel,
        out_shape=(
            jax.ShapeDtypeStruct((tc, bins, tr), bf16),
            jax.ShapeDtypeStruct((tr, width), bf16),
        ),
        in_specs=[any_spec()] * len(operands),
        out_specs=(full_spec(),) * 2,
        scratch_shapes=scratch,
        compiler_params=pltpu.CompilerParams(collective_id=0, has_side_effects=True),
    )(*operands)


def hand_over(distogram, seq_out):
    pieces = 4
    part = distogram.shape[0] // pieces

    def kernel(big_in, small_in, big_out, small_out, big, small, sem_in, sem_out):
        def moves(n):
            at = pl.ds(n * part, part)
            return (
                pltpu.make_async_copy(big_in.at[at], big.at[at], sem_in.at[n]),
                pltpu.make_async_copy(big.at[at], big_out.at[at], sem_out.at[n]),
            )

        steps = [moves(n) for n in range(pieces)] + [
            (
                pltpu.make_async_copy(small_in, small, sem_in.at[pieces]),
                pltpu.make_async_copy(small, small_out, sem_out.at[pieces]),
            )
        ]
        for take, _ in steps:
            take.start()
        for take, give in steps:
            take.wait()
            give.start()
        for _, give in steps:
            give.wait()

    arrays = (distogram, seq_out)
    shapes = [jax.ShapeDtypeStruct(x.shape, x.dtype) for x in arrays]
    return pl.pallas_call(
        kernel,
        out_shape=shapes,
        in_specs=[any_spec()] * 2,
        out_specs=[any_spec()] * 2,
        scratch_shapes=[pltpu.VMEM(x.shape, x.dtype) for x in arrays]
        + [pltpu.SemaphoreType.DMA((pieces + 1,))] * 2,
    )(*arrays)


def per_device(
    pair_state,
    seq_state,
    residue_index,
    residue_mask,
    position_table,
    attention_gain,
    bias_norm_gain,
    query_weight,
    key_weight,
    value_weight,
    gate_weight,
    out_weight,
    bias_weight,
    outer_gain,
    outer_weight,
    outer_out_weight,
    transition_gain,
    up_weight,
    down_weight,
    distance_weight,
):
    parts = pair_state.shape[0] // pair_state.shape[1]
    distogram, seq_out = trunk(
        pair_state,
        pair_state.reshape(parts, -1, pair_state.shape[2]),
        seq_state,
        residue_index,
        residue_mask,
        position_table,
        (attention_gain, bias_norm_gain, outer_gain, transition_gain),
        jnp.swapaxes(bias_weight, 1, 2),
        distance_weight.T,
        (
            query_weight,
            key_weight,
            value_weight,
            gate_weight,
            out_weight,
            outer_weight,
            outer_out_weight,
            up_weight,
            down_weight,
        ),
    )
    distogram, seq_out = hand_over(distogram, seq_out)
    return distogram.transpose(2, 0, 1), seq_out


def solution(mesh):
    heads_split = P(None, None, "col")
    in_specs = (
        (P("row", "col", None), P("row", "col"))
        + (P(),) * 5
        + (heads_split,) * 5
        + (P(),) * 8
    )
    out_specs = (P("row", "col", None), P("row", "col"))
    return jax.shard_map(
        per_device, mesh=mesh, in_specs=in_specs, out_specs=out_specs, check_vma=False
    )
```
